256 devices in a mesh: rows: 32 (over y, z), cols: 8 (over x, core).
Axes of the slice: x: 4, y: 4, z: 8, core: 2. Of those that a mesh axis runs over, the one named last changes fastest.
Arguments:
- genotypes: int32 [20480, 4096], P('rows', 'cols'), may hold values from 0 to 2
- frequencies: float32 [4096], P('cols'), may hold values from 0.05 to 0.5
- traits: bfloat16 [20480, 32768], P('rows', 'cols'), may hold values from -6 to 6
- geno_sketch: bfloat16 [4096, 512], P('cols'), may hold values from -0.09375 to 0.09375
- trait_sketch: bfloat16 [32768, 512], P('cols'), may hold values from -0.03125 to 0.03125
- initial: float32 [512, 256], replicated, may hold values from -6 to 6
Outputs:
- geno_scores: bfloat16 [20480, 256], P('rows')
- trait_scores: bfloat16 [20480, 256], P('rows')
- geno_loadings: float32 [256, 4096], P('rows', 'cols')
- trait_loadings: float32 [256, 32768], P('rows', 'cols')
The draws below stay inside these ranges and needn't reach their ends.
All inputs are finite; a program needn't handle non-finite values.
Results may differ from the reference program's by a relative error of at most 0.0059.
Values sent between devices are 32-bit elements; how exact they have to be, the bound alone decides.
A program may use at most 128 MiB of HBM per device.

```python
import math
import jax
import jax.numpy as jnp
from jax import lax

TRAITS = 32768
SKETCH = 512
PAIRS = 256
PEOPLE = 20480
GENO = 4096


def plant(array, key, least, top_value):
    longest = array.shape.index(max(array.shape))
    spots = []
    for shift in (0, 1):
        where = [jax.random.randint(jax.random.fold_in(key, axis), (), 0, length) for axis, length in enumerate(array.shape)]
        where[longest] = (where[longest] + shift) % array.shape[longest]
        spots.append(tuple(where))
    return array.at[spots[0]].set(least).at[spots[1]].set(top_value)


def shard_levels(own_key, extent, pieces, smallest, high):
    factor_of, own = 1.0, jax.random.fold_in(own_key, 6)
    for dim, shards_of in pieces:
        steps = jnp.exp(jax.random.uniform(jax.random.fold_in(own, dim), (shards_of,), jnp.float32, smallest / len(pieces), high / len(pieces)))
        factor_of = factor_of * jnp.repeat(steps, extent[dim] // shards_of).reshape([-1 if axis == dim else 1 for axis in range(len(extent))])
    return factor_of


def centred(own_key, dims, deviation, reach, cuts=(), kind=jnp.bfloat16):
    loudness = shard_levels(own_key, dims, cuts, -0.22, 0.18) if cuts else 1.0
    values = jax.random.normal(own_key, dims, jnp.float32) * deviation * loudness
    return jnp.minimum(jnp.maximum(values, -reach), reach).astype(kind)


def setup_inputs(seed: int = 0) -> dict:
    arg_keys = jax.random.split(jax.random.key(seed), 7)
    genotypes = plant(jax.random.randint(arg_keys[0], (PEOPLE, GENO), 0, 3), jax.random.fold_in(arg_keys[0], 1), 0, 2).astype(jnp.int32)
    frequencies = jnp.clip(jnp.exp(math.log(0.5) - 2.3025851 * jax.random.uniform(arg_keys[1], (GENO,), jnp.float32) ** shard_levels(arg_keys[1], (GENO,), ((0, 8),), -0.2, 0.2)), 0.05, 0.5)
    traits = centred(arg_keys[2], (PEOPLE, TRAITS), 1.0, 6.0, ((0, 32), (1, 8)))
    geno_sketch = centred(arg_keys[3], (GENO, SKETCH), GENO ** -0.5, 0.09375, ((0, 8),))
    trait_sketch = centred(arg_keys[4], (TRAITS, SKETCH), TRAITS ** -0.5, 0.03125, ((0, 8),))
    initial = centred(arg_keys[5], (SKETCH, PAIRS), 1.0, 6.0, (), jnp.float32)
    return {"genotypes": genotypes, "frequencies": frequencies, "traits": traits, "geno_sketch": geno_sketch, "trait_sketch": trait_sketch, "initial": initial}


def standard(genotypes, frequencies):
    spread = lax.rsqrt(2.0 * frequencies * (1.0 - frequencies))
    return ((genotypes.astype(jnp.float32) - 2.0 * frequencies) * spread).astype(jnp.bfloat16)

def unit_columns(matrix):
    return matrix * lax.rsqrt(lax.optimization_barrier(jnp.mean(matrix * matrix, axis=0, keepdims=True)) + 1e-06)

def make_basis(sketch_view):
    gram_view = jnp.dot(sketch_view.T, sketch_view, precision=lax.Precision.HIGHEST) / PEOPLE
    lower_view = jnp.linalg.cholesky(gram_view)
    return lax.linalg.triangular_solve(lower_view, sketch_view, left_side=False, lower=True, transpose_a=True)

def reference(genotypes, frequencies, traits, geno_sketch, trait_sketch, initial):
    standardized = standard(genotypes, frequencies)
    sketch_geno = jnp.dot(standardized.astype(jnp.float32), geno_sketch.astype(jnp.float32), preferred_element_type=jnp.float32)
    sketch_trait = jnp.dot(traits.astype(jnp.float32), trait_sketch.astype(jnp.float32), preferred_element_type=jnp.float32)
    basis_geno = make_basis(sketch_geno)
    basis_trait = make_basis(sketch_trait)
    crossed = jnp.dot(basis_geno.T, basis_trait, precision=lax.Precision.HIGHEST) / PEOPLE
    left_dirs = unit_columns(jnp.dot(crossed, initial, precision=lax.Precision.HIGHEST))
    right_dirs = unit_columns(jnp.dot(crossed.T, left_dirs, precision=lax.Precision.HIGHEST))
    root_sketch = math.sqrt(SKETCH)
    geno_scores = (jnp.dot(basis_geno, left_dirs, precision=lax.Precision.HIGHEST) / root_sketch).astype(jnp.bfloat16)
    trait_scores = (jnp.dot(basis_trait, right_dirs, precision=lax.Precision.HIGHEST) / root_sketch).astype(jnp.bfloat16)
    root_people = math.sqrt(PEOPLE)
    geno_loadings = jnp.dot(geno_scores.T.astype(jnp.float32), standardized.astype(jnp.float32), preferred_element_type=jnp.float32) / root_people
    trait_loadings = jnp.dot(trait_scores.T.astype(jnp.float32), traits.astype(jnp.float32), preferred_element_type=jnp.float32) / root_people
    return (geno_scores, trait_scores, geno_loadings, trait_loadings)
```

```python
import functools
import math

import jax
import jax.numpy as jnp
from jax import lax
from jax.experimental import pallas as pl
from jax.experimental.pallas import tpu as pltpu
from jax.sharding import PartitionSpec as P

HI=lax.Precision.HIGHEST
F32=jnp.float32
def dotf(a,b,ca,cb):
    return lax.dot_general(a,b,(((ca,),(cb,)),((),())),precision=HI,preferred_element_type=F32)

def factor(d_ref):
    row=lax.broadcasted_iota(jnp.int32,(8,1),0)
    for p in range(16):
        PA=[d_ref[m,8*p:8*p+8,0:128] for m in (0,1)]
        PI=[d_ref[m,8*p:8*p+8,128:256] for m in (0,1)]
        dv=[jnp.ones((8,1),F32) for m in (0,1)]
        for j in range(8):
            for m in (0,1):
                c=PA[m][:,8*p+j:8*p+j+1]
                d=c[j:j+1,:]
                dv[m]=jnp.where(row==j,d,dv[m])
                if j<7:
                    f=jnp.where(row>j,c*(1.0/d),0.0)
                    PI[m]=PI[m]-f*PI[m][j:j+1,:]
                    PA[m]=PA[m]-f*PA[m][j:j+1,:]
        T=[];U=[];V=[]
        for m in (0,1):
            s=lax.rsqrt(dv[m])
            U.append(PA[m]*s); V.append(PI[m]*s)
            d_ref[m,8*p:8*p+8,128:256]=V[m]
        if p<15:
            for m in (0,1): T.append(U[m].T)
            for g in range(p+1,16):
                for m in (0,1):
                    X=d_ref[m,8*g:8*g+8,0:128]; Y=d_ref[m,8*g:8*g+8,128:256]
                    for j in range(8):
                        t=T[m][8*g:8*g+8,j:j+1]
                        X=X-t*U[m][j:j+1,:]; Y=Y-t*V[m][j:j+1,:]
                    d_ref[m,8*g:8*g+8,0:128]=X; d_ref[m,8*g:8*g+8,128:256]=Y

def inverse_factors(a_ref,d_ref,load,fac=factor):
    eye=(lax.broadcasted_iota(jnp.int32,(128,128),0)==lax.broadcasted_iota(jnp.int32,(128,128),1)).astype(F32)
    load()
    for m in (0,1):
        a_ref[m,:,512:1024]=jnp.zeros((512,512),F32)
        for k in range(4): a_ref[m,128*k:128*k+128,512+128*k:640+128*k]=eye
    def body(k,_):
        for kk in range(4):
            @pl.when(k==kk)
            def _():
                for m in (0,1):
                    d_ref[m,:,0:128]=a_ref[m,128*kk:128*kk+128,128*kk:128*kk+128]
                    d_ref[m,:,128:256]=eye
        fac(d_ref)
        for kk in range(4):
            @pl.when(k==kk)
            def _():
                lo=128*(kk+1)
                for m in (0,1):
                    R=dotf(d_ref[m,:,128:256],a_ref[m,128*kk:128*kk+128,lo:lo+512],1,0)
                    a_ref[m,128*kk:128*kk+128,lo:lo+512]=R
                    if kk<3:
                        n=512-lo
                        a_ref[m,lo:512,lo:lo+512]=a_ref[m,lo:512,lo:lo+512]-dotf(R[:,:n].T,R,1,0)
        return 0
    lax.fori_loop(0,4,body,0)

def unit(v):
    return v*lax.rsqrt(jnp.mean(v*v,axis=0,keepdims=True)+1e-06)

def dirs_kernel(fac,gg,gt,cr,init,wg,wt,a_ref,d_ref):
    def load():
        a_ref[0,:,0:512]=gg[...]; a_ref[1,:,0:512]=gt[...]
    inverse_factors(a_ref,d_ref,load,fac)
    Mg=lambda: a_ref[0,:,512:1024]
    Mt=lambda: a_ref[1,:,512:1024]
    q=dotf(Mt(),init[...],0,0)
    u=dotf(cr[...],q,1,0)
    left=unit(dotf(Mg(),u,1,0))
    p=dotf(Mg(),left,0,0)
    v=dotf(cr[...],p,0,0)
    right=unit(dotf(Mt(),v,1,0))
    sc=1.0/math.sqrt(512.0)
    wg[...]=p*sc
    wt[...]=dotf(Mt(),right,0,0)*sc

def dirs(gg,gt,cr,init,fac=factor):
    vm=pl.BlockSpec(memory_space=pltpu.VMEM)
    return pl.pallas_call(functools.partial(dirs_kernel,fac),out_shape=[jax.ShapeDtypeStruct((512,256),F32)]*2,
      in_specs=[vm]*4,out_specs=[vm]*2,scratch_shapes=[pltpu.VMEM((2,512,1024),F32),pltpu.VMEM((2,128,256),F32)],
      compiler_params=pltpu.CompilerParams(vmem_limit_bytes=48<<20),name="dirs")(gg,gt,cr,init)


def standard(genotypes, frequencies):
    spread = lax.rsqrt(2.0 * frequencies * (1.0 - frequencies))
    return ((genotypes.astype(jnp.float32) - 2.0 * frequencies) * spread).astype(jnp.bfloat16)


def on_device(genotypes, frequencies, traits, geno_sketch, trait_sketch, initial):
    people = genotypes.shape[0] * lax.axis_size("rows")
    standardized = standard(genotypes, frequencies)
    partial_geno = jnp.dot(standardized, geno_sketch, preferred_element_type=jnp.float32)
    partial_trait = jnp.dot(traits, trait_sketch, preferred_element_type=jnp.float32)
    sketch_geno, sketch_trait = lax.psum((partial_geno, partial_trait), "cols")
    grams = lax.psum(
        (
            dotf(sketch_geno, sketch_geno, 0, 0),
            dotf(sketch_trait, sketch_trait, 0, 0),
            dotf(sketch_geno, sketch_trait, 0, 0),
        ),
        "rows",
    )
    weights_geno, weights_trait = dirs(*[g / people for g in grams], initial)
    geno_scores = jnp.dot(sketch_geno, weights_geno, precision=HI).astype(jnp.bfloat16)
    trait_scores = jnp.dot(sketch_trait, weights_trait, precision=HI).astype(jnp.bfloat16)
    geno_width = standardized.shape[1]
    geno_term = lax.dot_general(
        geno_scores, standardized, (((0,), (0,)), ((), ())), preferred_element_type=jnp.float32
    )
    trait_term = lax.dot_general(
        trait_scores, traits, (((0,), (0,)), ((), ())), preferred_element_type=jnp.float32
    )
    summed = lax.psum_scatter(
        jnp.concatenate([geno_term, trait_term], axis=1), "rows", scatter_dimension=0, tiled=True
    )
    root_people = math.sqrt(people)
    return (geno_scores, trait_scores, summed[:, :geno_width] / root_people, summed[:, geno_width:] / root_people)


def solution(mesh):
    placed = (
        P("rows", "cols"),
        P("cols"),
        P("rows", "cols"),
        P("cols", None),
        P("cols", None),
        P(),
    )
    return jax.shard_map(
        on_device,
        mesh=mesh,
        in_specs=placed,
        out_specs=(P("rows", None), P("rows", None), P("rows", "cols"), P("rows", "cols")),
        check_vma=False,
    )
```

```python
import functools
import math

import jax
import jax.numpy as jnp
from jax import lax
from jax.experimental import pallas as pl
from jax.experimental.pallas import tpu as pltpu
from jax.sharding import PartitionSpec as P

HI=lax.Precision.HIGHEST
F32=jnp.float32
def dotf(a,b,ca,cb):
    return lax.dot_general(a,b,(((ca,),(cb,)),((),())),precision=HI,preferred_element_type=F32)

def factor(d_ref):
    row=lax.broadcasted_iota(jnp.int32,(8,1),0)
    for p in range(16):
        PA=[d_ref[m,8*p:8*p+8,0:128] for m in (0,1)]
        PI=[d_ref[m,8*p:8*p+8,128:256] for m in (0,1)]
        dv=[jnp.ones((8,1),F32) for m in (0,1)]
        for j in range(8):
            for m in (0,1):
                c=PA[m][:,8*p+j:8*p+j+1]
                d=c[j:j+1,:]
                dv[m]=jnp.where(row==j,d,dv[m])
                if j<7:
                    f=jnp.where(row>j,c*(1.0/d),0.0)
                    PI[m]=PI[m]-f*PI[m][j:j+1,:]
                    PA[m]=PA[m]-f*PA[m][j:j+1,:]
        T=[];U=[];V=[]
        for m in (0,1):
            s=lax.rsqrt(dv[m])
            U.append(PA[m]*s); V.append(PI[m]*s)
            d_ref[m,8*p:8*p+8,128:256]=V[m]
        if p<15:
            for m in (0,1): T.append(U[m].T)
            for g in range(p+1,16):
                for m in (0,1):
                    X=d_ref[m,8*g:8*g+8,0:128]; Y=d_ref[m,8*g:8*g+8,128:256]
                    for j in range(8):
                        t=T[m][8*g:8*g+8,j:j+1]
                        X=X-t*U[m][j:j+1,:]; Y=Y-t*V[m][j:j+1,:]
                    d_ref[m,8*g:8*g+8,0:128]=X; d_ref[m,8*g:8*g+8,128:256]=Y

def inverse_factors(a_ref,d_ref,load,fac=factor):
    eye=(lax.broadcasted_iota(jnp.int32,(128,128),0)==lax.broadcasted_iota(jnp.int32,(128,128),1)).astype(F32)
    load()
    for m in (0,1):
        a_ref[m,:,512:1024]=jnp.zeros((512,512),F32)
        for k in range(4): a_ref[m,128*k:128*k+128,512+128*k:640+128*k]=eye
    def body(k,_):
        for kk in range(4):
            @pl.when(k==kk)
            def _():
                for m in (0,1):
                    d_ref[m,:,0:128]=a_ref[m,128*kk:128*kk+128,128*kk:128*kk+128]
                    d_ref[m,:,128:256]=eye
        fac(d_ref)
        for kk in range(4):
            @pl.when(k==kk)
            def _():
                lo=128*(kk+1)
                for m in (0,1):
                    R=dotf(d_ref[m,:,128:256],a_ref[m,128*kk:128*kk+128,lo:lo+512],1,0)
                    a_ref[m,128*kk:128*kk+128,lo:lo+512]=R
                    if kk<3:
                        n=512-lo
                        a_ref[m,lo:512,lo:lo+512]=a_ref[m,lo:512,lo:lo+512]-dotf(R[:,:n].T,R,1,0)
        return 0
    lax.fori_loop(0,4,body,0)

def unit(v):
    return v*lax.rsqrt(jnp.mean(v*v,axis=0,keepdims=True)+1e-06)

def dirs_kernel(fac,gg,gt,cr,init,wg,wt,a_ref,d_ref):
    def load():
        a_ref[0,:,0:512]=gg[...]; a_ref[1,:,0:512]=gt[...]
    inverse_factors(a_ref,d_ref,load,fac)
    Mg=lambda: a_ref[0,:,512:1024]
    Mt=lambda: a_ref[1,:,512:1024]
    q=dotf(Mt(),init[...],0,0)
    u=dotf(cr[...],q,1,0)
    left=unit(dotf(Mg(),u,1,0))
    p=dotf(Mg(),left,0,0)
    v=dotf(cr[...],p,0,0)
    right=unit(dotf(Mt(),v,1,0))
    sc=1.0/math.sqrt(512.0)
    wg[...]=p*sc
    wt[...]=dotf(Mt(),right,0,0)*sc

def dirs(gg,gt,cr,init,fac=factor):
    vm=pl.BlockSpec(memory_space=pltpu.VMEM)
    return pl.pallas_call(functools.partial(dirs_kernel,fac),out_shape=[jax.ShapeDtypeStruct((512,256),F32)]*2,
      in_specs=[vm]*4,out_specs=[vm]*2,scratch_shapes=[pltpu.VMEM((2,512,1024),F32),pltpu.VMEM((2,128,256),F32)],
      compiler_params=pltpu.CompilerParams(vmem_limit_bytes=48<<20),name="dirs")(gg,gt,cr,init)


MESH = pl.DeviceIdType.MESH


class Place:
    def __init__(self):
        rows, cols = lax.axis_index("rows"), lax.axis_index("cols")
        self.x, self.core = lax.div(cols, 2), lax.rem(cols, 2)
        self.y, self.z = lax.div(rows, 8), lax.rem(rows, 8)

    def ring(self, axis):
        return (self.z, 8) if axis == "z" else (getattr(self, axis), 4)

    def other(self, axis, step):
        here, size = self.ring(axis)
        return lax.rem(here + step + size, size)

    def device(self, axis, step):
        at = {"x": self.x, "y": self.y, "z": self.z, "core": self.core}
        at[axis] = 1 - self.core if axis == "core" else self.other(axis, step)
        return (at["y"] * 8 + at["z"], at["x"] * 2 + at["core"])


class Net:
    def __init__(self, place, sends, recvs):
        self.place, self.sends, self.recvs, self.count = place, sends, recvs, 0

    def greet(self, axes):
        barrier = pltpu.get_barrier_semaphore()
        partners = [(a, s) for a in axes for s in range(1, {"core": 2, "z": 8}.get(a, 4))]
        for axis, step in partners:
            pl.semaphore_signal(
                barrier, inc=1, device_id=self.place.device(axis, step), device_id_type=MESH
            )
        pl.semaphore_wait(barrier, len(partners))

    def send(self, source, target, axis, step=1):
        slot = self.count
        self.count += 1
        copy = pltpu.make_async_remote_copy(
            src_ref=source,
            dst_ref=target,
            send_sem=self.sends.at[slot],
            recv_sem=self.recvs.at[slot],
            device_id=self.place.device(axis, step),
            device_id_type=MESH,
        )
        copy.start()
        return copy

    def scatter(self, axis, part, landing):
        size = self.place.ring(axis)[1]
        order = sorted(range(1, size), key=lambda s: -min(s, size - s))
        return [
            self.send(part(self.place.other(axis, s)), landing.at[s - 1], axis, s) for s in order
        ]

    def gather(self, axis, own):
        size = self.place.ring(axis)[1]
        order = sorted(range(1, size), key=lambda s: -min(s, size - s))
        return [self.send(own, own, axis, s) for s in order]


def finish(copies):
    for copy in copies:
        copy.wait()


def rows_of(index, count):
    return pl.ds(pl.multiple_of(index * count, count), count)


def total_of(landing):
    total = landing[0]
    for s in range(1, landing.shape[0]):
        total = total + landing[s]
    return total


def gram_stream(net, axes, source, land1, part1, land2, part2, land3, out3, out2, out1):
    place = net.place
    first, second = axes
    i1, i2, z = place.ring(first)[0], place.ring(second)[0], place.z
    copies = net.scatter(first, lambda i: source.at[rows_of(i, 288)], land1)
    yield
    finish(copies)
    part1[...] = source[rows_of(i1, 288)] + total_of(land1)
    copies = net.scatter(second, lambda i: part1.at[rows_of(i, 72)], land2)
    part2[72:128] = jnp.zeros((56, 128), F32)
    yield
    finish(copies)
    part2[0:72] = part1[rows_of(i2, 72)] + total_of(land2)
    copies = net.scatter("z", lambda i: part2.at[rows_of(i, 16)], land3)
    yield
    finish(copies)
    out3[rows_of(z, 16)] = part2[rows_of(z, 16)] + total_of(land3)
    copies = net.gather("z", out3.at[rows_of(z, 16)])
    yield
    finish(copies)
    out2[i2] = out3[0:72]
    copies = net.gather(second, out2.at[i2])
    yield
    finish(copies)
    out1[i1] = out2[...]
    copies = net.gather(first, out1.at[i1])
    yield
    finish(copies)


GRAM_SCRATCH = [
    pltpu.VMEM((3, 288, 128), F32),
    pltpu.VMEM((288, 128), F32),
    pltpu.VMEM((3, 72, 128), F32),
    pltpu.VMEM((128, 128), F32),
    pltpu.VMEM((7, 16, 128), F32),
    pltpu.VMEM((128, 128), F32),
    pltpu.VMEM((4, 72, 128), F32),
    pltpu.VMEM((4, 4, 72, 128), F32),
]
UPPER = [(i, j) for j in range(4) for i in range(j + 1)]


def together(streams):
    streams = list(streams)
    while streams:
        alive = []
        for stream in streams:
            try:
                next(stream)
                alive.append(stream)
            except StopIteration:
                pass
        streams = alive


def sketch_kernel(people, geno, shift, spread, traits, gsk, tsk, gg, gt, cr, own, std, *scratch):
    give, take, held, land, both, source, final = scratch[:7]
    alpha, beta = scratch[7:15], scratch[15:23]
    place = Place()
    net = Net(place, scratch[23], scratch[24])
    x, k = place.x, place.core
    std[...] = ((geno[...].astype(F32) - shift[...]) * spread[...]).astype(jnp.bfloat16)

    def piece(half, j):
        rows = rows_of(half, 320)
        if j < 2:
            return jnp.dot(std[rows], gsk[:, 256 * j : 256 * j + 256], preferred_element_type=F32)
        j -= 2
        return jnp.dot(traits[rows], tsk[:, 256 * j : 256 * j + 256], preferred_element_type=F32)

    net.greet(("core", "x", "y", "z"))
    copies = []
    for j in (2, 3, 0, 1):
        give[j] = piece(1 - k, j)
        copies.append(net.send(give.at[j], take.at[j], "core"))
    for j in (2, 3, 0, 1):
        held[j] = piece(k, j)
    for j, copy in zip((2, 3, 0, 1), copies):
        copy.wait()
        held[j] = held[j] + take[j]
    finish(net.scatter("x", lambda i: held.at[:, rows_of(i, 80)], land))
    for j in range(4):
        mine = held[j, rows_of(x, 80)]
        for s in range(3):
            mine = mine + land[s, j]
        both[k, :, 256 * j : 256 * j + 256] = mine
    copy = net.send(both.at[k], both.at[k], "core")
    own[...] = both[k]
    copy.wait()
    flat = both[...].reshape(160, 1024)
    view = both[:, :, pl.ds(pl.multiple_of(512 * k, 512), 512)].reshape(160, 512)
    side = both[:, :, pl.ds(pl.multiple_of(512 + 256 * k, 256), 256)].reshape(160, 256)
    gram = dotf(view.T, view, 1, 0)
    for t, (i, j) in enumerate(UPPER):
        source[128 * t : 128 * t + 128] = gram[128 * i : 128 * i + 128, 128 * j : 128 * j + 128]
    cross = dotf(flat[:, 0:512].T, side, 1, 0)
    for j in range(2):
        for i in range(4):
            t = 10 + 4 * j + i
            source[128 * t : 128 * t + 128] = cross[128 * i : 128 * i + 128, 128 * j : 128 * j + 128]
    together(
        [
            gram_stream(net, ("x", "y"), source.at[0:1152], *alpha),
            gram_stream(net, ("y", "x"), source.at[1152:2304], *beta),
        ]
    )
    for s, stream in enumerate((alpha, beta)):
        for i in range(4):
            for j in range(4):
                at = 1152 * s + 288 * i + 72 * j
                final[k, at : at + 72] = stream[7][i, j]
    net.send(final.at[k], final.at[k], "core").wait()
    scale = 1.0 / people
    for v, gram_out in enumerate((gg, gt)):
        gram_out[...] = jnp.zeros((512, 512), F32)
        for t, (i, j) in enumerate(UPPER):
            gram_out[128 * i : 128 * i + 128, 128 * j : 128 * j + 128] = (
                final[v, 128 * t : 128 * t + 128] * scale
            )
        for j in range(2):
            for i in range(4):
                t, at = 10 + 4 * j + i, 256 * v + 128 * j
                cr[128 * i : 128 * i + 128, at : at + 128] = final[v, 128 * t : 128 * t + 128] * scale


def sketches(people, geno, shift, spread, traits, gsk, tsk):
    vm = pl.BlockSpec(memory_space=pltpu.VMEM)
    square = jax.ShapeDtypeStruct((512, 512), F32)
    sems = 4 + 3 + 1 + 2 * (2 * (3 + 3 + 7)) + 1
    return pl.pallas_call(
        functools.partial(sketch_kernel, people),
        out_shape=[
            square,
            square,
            square,
            jax.ShapeDtypeStruct((80, 1024), F32),
            jax.ShapeDtypeStruct((640, 512), jnp.bfloat16),
        ],
        in_specs=[vm] * 6,
        out_specs=[vm] * 5,
        scratch_shapes=[
            pltpu.VMEM((4, 320, 256), F32),
            pltpu.VMEM((4, 320, 256), F32),
            pltpu.VMEM((4, 320, 256), F32),
            pltpu.VMEM((3, 4, 80, 256), F32),
            pltpu.VMEM((2, 80, 1024), F32),
            pltpu.VMEM((2304, 128), F32),
            pltpu.VMEM((2, 2304, 128), F32),
            *GRAM_SCRATCH,
            *GRAM_SCRATCH,
            pltpu.SemaphoreType.DMA((sems,)),
            pltpu.SemaphoreType.DMA((sems,)),
        ],
        compiler_params=pltpu.CompilerParams(
            collective_id=1, has_side_effects=True, vmem_limit_bytes=56 << 20
        ),
        name="sketches",
    )(geno, shift, spread, traits, gsk, tsk)


def rows_first(net, source, land1, part1, land2, out):
    place = net.place
    copies = net.scatter("y", lambda i: source.at[i], land1)
    yield
    finish(copies)
    part1[...] = source[place.y] + total_of(land1)
    copies = net.scatter("z", lambda i: part1.at[i], land2)
    yield
    finish(copies)
    out[...] = part1[place.z] + total_of(land2)


def ring_first(net, source, lands, part1, land2, out):
    place = net.place
    half = source.shape[-1] // 2
    spans = (slice(0, half), slice(half, 2 * half))
    arriving = {}
    for d, step in enumerate((1, 7)):
        far = place.other("z", 4)
        arriving[d] = [
            net.send(source.at[:, far, :, spans[d]], lands.at[d, 0, :, :, spans[d]], "z", step)
        ]
    yield
    sent = []
    for hop in (1, 2, 3):
        leaving = {0: [], 1: []}
        for part in (0, 1):
            for d, step in enumerate((1, 7)):
                turn = 4 - hop if d == 0 else 4 + hop
                chunk = place.other("z", turn)
                passed = lands.at[d, hop - 1]
                if hop == 1:
                    if part == 0:
                        arriving[d][0].wait_recv()
                        sent.append(arriving[d][0])
                        passed[:, :, spans[d]] = passed[:, :, spans[d]] + source[:, chunk, :, spans[d]]
                        origin = passed.at[:, :, spans[d]]
                        which = d
                    else:
                        origin = source.at[:, chunk, :, spans[1 - d]]
                        which = 1 - d
                else:
                    which = d if part == 0 else 1 - d
                    arriving[d][part].wait_recv()
                    sent.append(arriving[d][part])
                    passed[:, :, spans[which]] = (
                        passed[:, :, spans[which]] + source[:, chunk, :, spans[which]]
                    )
                    origin = passed.at[:, :, spans[which]]
                leaving[d].append(
                    net.send(origin, lands.at[d, hop, :, :, spans[which]], "z", step)
                )
        arriving = leaving
        yield
    for d in (0, 1):
        for copy in arriving[d]:
            copy.wait_recv()
            sent.append(copy)
    for copy in sent:
        copy.wait_send()
    part1[...] = source[:, place.z] + lands[0, 3] + lands[1, 3]
    copies = net.scatter("y", lambda i: part1.at[i], land2)
    yield
    finish(copies)
    out[...] = part1[place.y] + total_of(land2)


def loading_kernel(people, own, wg, wt, std, traits, gsc, tsc, gl, tl, *scratch):
    score, left, right = scratch[:3]
    alpha, beta = scratch[3:7], scratch[7:11]
    place = Place()
    net = Net(place, scratch[11], scratch[12])
    x, k = place.x, place.core
    score[k, x, :, 0:256] = dotf(own[:, 0:512], wg[...], 1, 0).astype(jnp.bfloat16).astype(F32)
    score[k, x, :, 256:512] = dotf(own[:, 512:1024], wt[...], 1, 0).astype(jnp.bfloat16).astype(F32)
    net.greet(("core", "x", "y", "z"))
    mine = score.at[k, x]
    across = [net.send(mine, mine, "x", s) for s in (2, 1, 3)]
    pair = [net.send(mine, mine, "core")]
    for s, copy in zip((2, 1, 3), across):
        copy.wait()
        came = score.at[k, place.other("x", -s)]
        pair.append(net.send(came, came, "core"))
    finish(pair)
    full = score[...].reshape(640, 512).astype(jnp.bfloat16)
    gsc[...] = full[:, 0:256]
    tsc[...] = full[:, 256:512]
    geno_t, trait_t = full[:, 0:256].T, full[:, 256:512].T

    def put(target, at, lhs, rhs):
        width = rhs.shape[1]
        target[:, :, :, at : at + width] = jnp.dot(lhs, rhs, preferred_element_type=F32).reshape(
            4, 8, 8, width
        )

    for at in range(0, 1792, 256):
        put(right, at, trait_t, traits[:, 2304 + at : 2560 + at])
    for at in range(0, 512, 256):
        put(right, 1792 + at, geno_t, std[:, at : at + 256])
    second = ring_first(net, right, *beta)
    next(second)
    for at in range(0, 2304, 256):
        put(left, at, trait_t, traits[:, at : at + 256])
    together([rows_first(net, left, *alpha), second])
    scale = 1.0 / math.sqrt(people)
    tl[:, 0:2304] = alpha[3][...] * scale
    tl[:, 2304:4096] = beta[3][:, 0:1792] * scale
    gl[...] = beta[3][:, 1792:2304] * scale


def loadings(people, own, wg, wt, std, traits):
    vm = pl.BlockSpec(memory_space=pltpu.VMEM)
    sems = 3 + 4 + 10 + 14 + 3
    return pl.pallas_call(
        functools.partial(loading_kernel, people),
        out_shape=[
            jax.ShapeDtypeStruct((640, 256), jnp.bfloat16),
            jax.ShapeDtypeStruct((640, 256), jnp.bfloat16),
            jax.ShapeDtypeStruct((8, 512), F32),
            jax.ShapeDtypeStruct((8, 4096), F32),
        ],
        in_specs=[vm] * 5,
        out_specs=[vm] * 4,
        scratch_shapes=[
            pltpu.VMEM((2, 4, 80, 512), F32),
            pltpu.VMEM((4, 8, 8, 2304), F32),
            pltpu.VMEM((4, 8, 8, 2304), F32),
            pltpu.VMEM((3, 8, 8, 2304), F32),
            pltpu.VMEM((8, 8, 2304), F32),
            pltpu.VMEM((7, 8, 2304), F32),
            pltpu.VMEM((8, 2304), F32),
            pltpu.VMEM((2, 4, 4, 8, 2304), F32),
            pltpu.VMEM((4, 8, 2304), F32),
            pltpu.VMEM((3, 8, 2304), F32),
            pltpu.VMEM((8, 2304), F32),
            pltpu.SemaphoreType.DMA((sems,)),
            pltpu.SemaphoreType.DMA((sems,)),
        ],
        compiler_params=pltpu.CompilerParams(
            collective_id=2, has_side_effects=True, vmem_limit_bytes=56 << 20
        ),
        name="loadings",
    )(own, wg, wt, std, traits)


def on_device(genotypes, frequencies, traits, geno_sketch, trait_sketch, initial):
    people = genotypes.shape[0] * lax.axis_size("rows")
    shift = (2.0 * frequencies)[None, :]
    spread = lax.rsqrt(2.0 * frequencies * (1.0 - frequencies))[None, :]
    gg, gt, cr, own, std = sketches(
        people, genotypes, shift, spread, traits, geno_sketch, trait_sketch
    )
    weights_geno, weights_trait = dirs(gg, gt, cr, initial)
    return tuple(loadings(people, own, weights_geno, weights_trait, std, traits))


def solution(mesh):
    placed = (
        P("rows", "cols"),
        P("cols"),
        P("rows", "cols"),
        P("cols", None),
        P("cols", None),
        P(),
    )
    return jax.shard_map(
        on_device,
        mesh=mesh,
        in_specs=placed,
        out_specs=(P("rows", None), P("rows", None), P("rows", "cols"), P("rows", "cols")),
        check_vma=False,
    )
```

```python
import functools
import math

import jax
import jax.numpy as jnp
from jax import lax
from jax.experimental import pallas as pl
from jax.experimental.pallas import tpu as pltpu
from jax.sharding import PartitionSpec as P

HI=lax.Precision.HIGHEST
F32=jnp.float32
def dotf(a,b,ca,cb):
    return lax.dot_general(a,b,(((ca,),(cb,)),((),())),precision=HI,preferred_element_type=F32)


def factor(d_ref):
    row = lax.broadcasted_iota(jnp.int32, (8, 128), 0)
    for p in range(16):
        rows = slice(8 * p, 8 * p + 8)
        gram, inverse = d_ref[rows, 0:128], d_ref[rows, 128:256]
        cell = {}
        for j in range(8):
            column = jnp.broadcast_to(gram[:, 8 * p + j : 8 * p + j + 1], (8, 128))
            for i in range(j, 8):
                cell[i, j] = column[i : i + 1, :]
        scales = []
        for j in range(8):
            scales.append(lax.rsqrt(cell[j, j]))
            if j == 7:
                break
            inv = 1.0 / cell[j, j]
            ratio = {i: cell[i, j] * inv for i in range(j + 1, 8)}
            for b in range(j + 1, 8):
                for i in range(b, 8):
                    cell[i, b] = cell[i, b] - ratio[i] * cell[b, j]
            factors = jnp.zeros((8, 128), F32)
            for i in range(j + 1, 8):
                factors = jnp.where(row == i, jnp.broadcast_to(ratio[i], (8, 128)), factors)
            inverse = inverse - factors * inverse[j : j + 1, :]
            gram = gram - factors * gram[j : j + 1, :]
        scale = jnp.broadcast_to(scales[0], (8, 128))
        for i in range(1, 8):
            scale = jnp.where(row == i, jnp.broadcast_to(scales[i], (8, 128)), scale)
        upper, under = gram * scale, inverse * scale
        d_ref[rows, 128:256] = under
        if p < 15:
            turned = upper.T
            for g in range(p + 1, 16):
                group = slice(8 * g, 8 * g + 8)
                left, right = d_ref[group, 0:128], d_ref[group, 128:256]
                for j in range(8):
                    times = turned[group, j : j + 1]
                    left = left - times * upper[j : j + 1, :]
                    right = right - times * under[j : j + 1, :]
                d_ref[group, 0:128] = left
                d_ref[group, 128:256] = right


def inverse_kernel(gram, out, a_ref, d_ref):
    eye = (
        lax.broadcasted_iota(jnp.int32, (128, 128), 0) == lax.broadcasted_iota(jnp.int32, (128, 128), 1)
    ).astype(F32)
    a_ref[:, 0:512] = gram[...]
    a_ref[:, 512:1024] = jnp.zeros((512, 512), F32)
    for k in range(4):
        a_ref[128 * k : 128 * k + 128, 512 + 128 * k : 640 + 128 * k] = eye

    def body(k, _):
        for kk in range(4):

            @pl.when(k == kk)
            def _():
                d_ref[:, 0:128] = a_ref[128 * kk : 128 * kk + 128, 128 * kk : 128 * kk + 128]
                d_ref[:, 128:256] = eye

        factor(d_ref)
        for kk in range(4):

            @pl.when(k == kk)
            def _():
                lo = 128 * (kk + 1)
                block = slice(128 * kk, 128 * kk + 128)
                panel = dotf(d_ref[:, 128:256], a_ref[block, lo : lo + 512], 1, 0)
                a_ref[block, lo : lo + 512] = panel
                if kk < 3:
                    a_ref[lo:512, lo : lo + 512] = a_ref[lo:512, lo : lo + 512] - dotf(
                        panel[:, : 512 - lo].T, panel, 1, 0
                    )

        return 0

    lax.fori_loop(0, 4, body, 0)
    out[...] = a_ref[:, 512:1024]


def inverse_factor(gram):
    vm = pl.BlockSpec(memory_space=pltpu.VMEM)
    return pl.pallas_call(
        inverse_kernel,
        out_shape=jax.ShapeDtypeStruct((512, 512), F32),
        in_specs=[vm],
        out_specs=vm,
        scratch_shapes=[pltpu.VMEM((512, 1024), F32), pltpu.VMEM((128, 256), F32)],
        compiler_params=pltpu.CompilerParams(vmem_limit_bytes=32 << 20),
        name="inverse_factor",
    )(gram)


MESH = pl.DeviceIdType.MESH


class Place:
    def __init__(self):
        rows, cols = lax.axis_index("rows"), lax.axis_index("cols")
        self.x, self.core = lax.div(cols, 2), lax.rem(cols, 2)
        self.y, self.z = lax.div(rows, 8), lax.rem(rows, 8)

    def ring(self, axis):
        return (self.z, 8) if axis == "z" else (getattr(self, axis), 4)

    def other(self, axis, step):
        here, size = self.ring(axis)
        return lax.rem(here + step + size, size)

    def device(self, axis, step):
        at = {"x": self.x, "y": self.y, "z": self.z, "core": self.core}
        at[axis] = 1 - self.core if axis == "core" else self.other(axis, step)
        return (at["y"] * 8 + at["z"], at["x"] * 2 + at["core"])


class Net:
    def __init__(self, place, sends, recvs):
        self.place, self.sends, self.recvs, self.count = place, sends, recvs, 0

    def greet(self, axes):
        barrier = pltpu.get_barrier_semaphore()
        partners = [(a, s) for a in axes for s in range(1, {"core": 2, "z": 8}.get(a, 4))]
        for axis, step in partners:
            pl.semaphore_signal(
                barrier, inc=1, device_id=self.place.device(axis, step), device_id_type=MESH
            )
        pl.semaphore_wait(barrier, len(partners))

    def send(self, source, target, axis, step=1):
        slot = self.count
        self.count += 1
        copy = pltpu.make_async_remote_copy(
            src_ref=source,
            dst_ref=target,
            send_sem=self.sends.at[slot],
            recv_sem=self.recvs.at[slot],
            device_id=self.place.device(axis, step),
            device_id_type=MESH,
        )
        copy.start()
        return copy

    def scatter(self, axis, part, landing):
        size = self.place.ring(axis)[1]
        order = sorted(range(1, size), key=lambda s: -min(s, size - s))
        return [
            self.send(part(self.place.other(axis, s)), landing.at[s - 1], axis, s) for s in order
        ]

    def gather(self, axis, own):
        size = self.place.ring(axis)[1]
        order = sorted(range(1, size), key=lambda s: -min(s, size - s))
        return [self.send(own, own, axis, s) for s in order]


def ring_scatter(net, axis, part, lands):
    place = net.place
    size = place.ring(axis)[1]
    turns = size // 2
    ways = ((0, 1), (1, size - 1))
    flight = {d: {d: net.send(part(place.other(axis, turns), d), lands(d, 0, d), axis, s)} for d, s in ways}
    sent = [flight[d][d] for d, _ in ways]
    for hop in range(1, turns):
        leaving = {0: {}, 1: {}}
        if hop == 1:
            for d, s in ways:
                chunk = place.other(axis, turns - 1 if d == 0 else 1 - turns)
                leaving[d][1 - d] = net.send(part(chunk, 1 - d), lands(d, 1, 1 - d), axis, s)
        yield
        for first in (True, False):
            for d, s in ways:
                h = d if first else 1 - d
                if h not in flight[d]:
                    continue
                chunk = place.other(axis, turns - hop if d == 0 else hop - turns)
                flight[d][h].wait_recv()
                passed, mine = lands(d, hop - 1, h), part(chunk, h)
                passed[...] = passed[...] + mine[...]
                leaving[d][h] = net.send(passed, lands(d, hop, h), axis, s)
        flight = leaving
        sent += [flight[d][h] for d in (0, 1) for h in (0, 1)]
    yield
    for d, _ in ways:
        for h in (0, 1):
            flight[d][h].wait_recv()
    for copy in sent:
        copy.wait_send()


def finish(copies):
    for copy in copies:
        copy.wait()


def rows_of(index, count):
    return pl.ds(pl.multiple_of(index * count, count), count)


def total_of(landing):
    total = landing[0]
    for s in range(1, landing.shape[0]):
        total = total + landing[s]
    return total


def gram_stream(net, axes, source, land1, part1, land2, part2, land3, out3, out2, out1):
    place = net.place
    first, second = axes
    i1, i2, z = place.ring(first)[0], place.ring(second)[0], place.z
    copies = net.scatter(first, lambda i: source.at[rows_of(i, 288)], land1)
    yield
    finish(copies)
    part1[...] = source[rows_of(i1, 288)] + total_of(land1)
    copies = net.scatter(second, lambda i: part1.at[rows_of(i, 72)], land2)
    part2[72:128] = jnp.zeros((56, 128), F32)
    yield
    finish(copies)
    part2[0:72] = part1[rows_of(i2, 72)] + total_of(land2)
    copies = net.scatter("z", lambda i: part2.at[rows_of(i, 16)], land3)
    yield
    finish(copies)
    out3[rows_of(z, 16)] = part2[rows_of(z, 16)] + total_of(land3)
    copies = net.gather("z", out3.at[rows_of(z, 16)])
    yield
    finish(copies)
    out2[i2] = out3[0:72]
    copies = net.gather(second, out2.at[i2])
    yield
    finish(copies)
    out1[i1] = out2[...]
    copies = net.gather(first, out1.at[i1])
    yield
    finish(copies)


GRAM_SCRATCH = [
    pltpu.VMEM((3, 288, 128), F32),
    pltpu.VMEM((288, 128), F32),
    pltpu.VMEM((3, 72, 128), F32),
    pltpu.VMEM((128, 128), F32),
    pltpu.VMEM((7, 16, 128), F32),
    pltpu.VMEM((128, 128), F32),
    pltpu.VMEM((4, 72, 128), F32),
    pltpu.VMEM((4, 4, 72, 128), F32),
]
UPPER = [(i, j) for j in range(4) for i in range(j + 1)]


def together(streams):
    streams = list(streams)
    while streams:
        alive = []
        for stream in streams:
            try:
                next(stream)
                alive.append(stream)
            except StopIteration:
                pass
        streams = alive


def share_sketch(net, full, mine):
    place = net.place
    yield
    here = full.at[mine]
    across = [net.send(here, here, "x", s) for s in (2, 1, 3)]
    yield
    yield
    yield
    yield
    pair = []
    for s, copy in zip((2, 1, 3), across):
        copy.wait()
        came = full.at[place.core * 4 + place.other("x", -s)]
        pair.append(net.send(came, came, "core"))
    yield
    finish(pair)


def sketch_kernel(people, geno, shift, spread, traits, gsk, tsk, gram_out, cross_out, full, std, *scratch):
    give, take, held, lands, both, source = scratch[:6]
    alpha, beta = scratch[6:14], scratch[14:22]
    place = Place()
    net = Net(place, scratch[22], scratch[23])
    x, k = place.x, place.core
    std[...] = ((geno[...].astype(F32) - shift[...]) * spread[...]).astype(jnp.bfloat16)

    def piece(half, j):
        rows = rows_of(half, 320)
        if j < 2:
            return jnp.dot(traits[rows], tsk[:, 256 * j : 256 * j + 256], preferred_element_type=F32)
        j -= 2
        return jnp.dot(std[rows], gsk[:, 256 * j : 256 * j + 256], preferred_element_type=F32)

    net.greet(("core", "x", "y", "z"))
    copies = []
    for j in range(4):
        give[j] = piece(1 - k, j)
        copies.append(net.send(give.at[j], take.at[j], "core"))

    def part(j, step):
        return held.at[j, rows_of(place.other("x", step), 80)]

    far, near = [], []
    for j in range(4):
        mine = piece(k, j)
        copies[j].wait()
        held[j] = mine + take[j]
        toward, away = (1, 3) if j < 2 else (3, 1)
        far.append(net.send(part(j, 2), lands.at[0, j], "x", toward))
        near.append(net.send(part(j, away), lands.at[1, j], "x", away))
    passing = []
    for j in range(4):
        toward = 1 if j < 2 else 3
        far[j].wait_recv()
        lands[0, j] = lands[0, j] + part(j, toward)[...]
        passing.append(net.send(lands.at[0, j], lands.at[2, j], "x", toward))
    for j in range(4):
        near[j].wait_recv()
        passing[j].wait_recv()
        at = 512 + 256 * j if j < 2 else 256 * j - 512
        both[k, :, at : at + 256] = part(j, 0)[...] + lands[1, j] + lands[2, j]
    copy = net.send(both.at[k], both.at[k], "core")
    full[k * 4 + x] = both[k]
    for other in far + near + passing:
        other.wait_send()
    copy.wait()
    full[(1 - k) * 4 + x] = both[1 - k]
    flat = both[...].reshape(160, 1024)
    view = both[:, :, pl.ds(pl.multiple_of(512 * k, 512), 512)].reshape(160, 512)
    side = both[:, :, pl.ds(pl.multiple_of(512 + 256 * k, 256), 256)].reshape(160, 256)
    gram = dotf(view.T, view, 1, 0)
    for t, (i, j) in enumerate(UPPER):
        source[128 * t : 128 * t + 128] = gram[128 * i : 128 * i + 128, 128 * j : 128 * j + 128]
    cross = dotf(flat[:, 0:512].T, side, 1, 0)
    for j in range(2):
        for i in range(4):
            t = 10 + 4 * j + i
            source[128 * t : 128 * t + 128] = cross[128 * i : 128 * i + 128, 128 * j : 128 * j + 128]
    together(
        [
            gram_stream(net, ("x", "y"), source.at[0:1152], *alpha),
            gram_stream(net, ("y", "x"), source.at[1152:2304], *beta),
            share_sketch(net, full, k * 4 + x),
        ]
    )
    for s, stream in enumerate((alpha, beta)):
        for i in range(4):
            for j in range(4):
                at = 1152 * s + 288 * i + 72 * j
                source[at : at + 72] = stream[7][i, j]
    scale = 1.0 / people
    gram_out[...] = jnp.zeros((512, 512), F32)
    for t, (i, j) in enumerate(UPPER):
        gram_out[128 * i : 128 * i + 128, 128 * j : 128 * j + 128] = source[128 * t : 128 * t + 128] * scale
    for j in range(2):
        for i in range(4):
            t = 10 + 4 * j + i
            cross_out[128 * i : 128 * i + 128, 128 * j : 128 * j + 128] = source[128 * t : 128 * t + 128] * scale


def sketches(people, geno, shift, spread, traits, gsk, tsk):
    vm = pl.BlockSpec(memory_space=pltpu.VMEM)
    sems = 4 + 12 + 1 + 2 * (2 * (3 + 3 + 7)) + 6
    return pl.pallas_call(
        functools.partial(sketch_kernel, people),
        out_shape=[
            jax.ShapeDtypeStruct((512, 512), F32),
            jax.ShapeDtypeStruct((512, 256), F32),
            jax.ShapeDtypeStruct((8, 80, 1024), F32),
            jax.ShapeDtypeStruct((640, 512), jnp.bfloat16),
        ],
        in_specs=[vm] * 6,
        out_specs=[vm] * 4,
        scratch_shapes=[
            pltpu.VMEM((4, 320, 256), F32),
            pltpu.VMEM((4, 320, 256), F32),
            pltpu.VMEM((4, 320, 256), F32),
            pltpu.VMEM((3, 4, 80, 256), F32),
            pltpu.VMEM((2, 80, 1024), F32),
            pltpu.VMEM((2304, 128), F32),
            *GRAM_SCRATCH,
            *GRAM_SCRATCH,
            pltpu.SemaphoreType.DMA((sems,)),
            pltpu.SemaphoreType.DMA((sems,)),
        ],
        compiler_params=pltpu.CompilerParams(
            collective_id=1, has_side_effects=True, vmem_limit_bytes=56 << 20
        ),
        name="sketches",
    )(geno, shift, spread, traits, gsk, tsk)


def unit(v):
    return v * lax.rsqrt(jnp.mean(v * v, axis=0, keepdims=True) + 1e-06)


def rows_first(net, source, land1, part1, land2, out):
    place, half = net.place, source.shape[-1] // 2
    yield from ring_scatter(
        net,
        "y",
        lambda i, h: source.at[i, :, :, half * h : half * h + half],
        lambda d, hop, h: land1.at[d, hop, :, :, half * h : half * h + half],
    )
    part1[...] = source[place.y] + land1[0, 1] + land1[1, 1]
    copies = net.scatter("z", lambda i: part1.at[i], land2)
    yield
    finish(copies)
    out[...] = part1[place.z] + total_of(land2)


def ring_first(net, source, land1, part1, land2, out):
    place, half = net.place, source.shape[-1] // 2
    yield from ring_scatter(
        net,
        "z",
        lambda i, h: source.at[:, i, :, half * h : half * h + half],
        lambda d, hop, h: land1.at[d, hop, :, :, half * h : half * h + half],
    )
    part1[...] = source[:, place.z] + land1[0, 3] + land1[1, 3]
    copies = net.scatter("y", lambda i: part1.at[i], land2)
    yield
    finish(copies)
    out[...] = part1[place.y] + total_of(land2)


def rows_scratch(width):
    return [
        pltpu.VMEM((4, 8, 8, width), F32),
        pltpu.VMEM((2, 2, 8, 8, width), F32),
        pltpu.VMEM((8, 8, width), F32),
        pltpu.VMEM((7, 8, width), F32),
        pltpu.VMEM((8, width), F32),
    ]


def ring_scratch(width):
    return [
        pltpu.VMEM((4, 8, 8, width), F32),
        pltpu.VMEM((2, 4, 4, 8, width), F32),
        pltpu.VMEM((4, 8, width), F32),
        pltpu.VMEM((3, 8, width), F32),
        pltpu.VMEM((8, width), F32),
    ]


STREAMS = (
    (rows_first, rows_scratch, 0, 1024, 0),
    (ring_first, ring_scratch, 1024, 1024, 0),
    (rows_first, rows_scratch, 2048, 1280, 0),
    (ring_first, ring_scratch, 3328, 768, 512),
)


def loading_kernel(people, inv_own, cross_own, init, sketch, std, traits, gsc, tsc, gl, tl, *scratch):
    inv, cross, people_traits = scratch[:3]
    parts = [scratch[3 + 5 * s : 8 + 5 * s] for s in range(4)]
    sends, recvs, loaded = scratch[23:26]
    place = Place()
    net = Net(place, sends, recvs)
    k = place.core
    load = pltpu.make_async_copy(traits, people_traits, loaded)
    load.start()
    net.greet(("core", "x", "y", "z"))
    cols = pl.ds(pl.multiple_of(256 * k, 256), 256)
    pair = []
    for i in range(4):
        block = (slice(128 * i, 128 * i + 128), slice(0, 128 * i + 128))
        pair.append(net.send(inv_own.at[block], inv.at[(k, *block)], "core"))
    pair.append(net.send(cross_own, cross.at[:, cols], "core"))
    inv[k] = inv_own[...]
    for i in range(3):
        inv[1 - k, 128 * i : 128 * i + 128, 128 * i + 128 : 512] = jnp.zeros((128, 384 - 128 * i), F32)
    cross[:, cols] = cross_own[...]
    finish(pair)
    left = unit(dotf(inv[0], dotf(cross[...], dotf(inv[1], init[...], 0, 0), 1, 0), 1, 0))
    scale = 1.0 / math.sqrt(inv.shape[1])
    geno_weights = dotf(inv[0], left, 0, 0)
    right = unit(dotf(inv[1], dotf(cross[...], geno_weights, 0, 0), 1, 0))
    trait_weights = dotf(inv[1], right, 0, 0)
    flat = sketch[...].reshape(640, 1024)
    tscore = dotf(flat[:, 512:1024], trait_weights * scale, 1, 0).astype(jnp.bfloat16)
    tsc[...] = tscore
    gscore = dotf(flat[:, 0:512], geno_weights * scale, 1, 0).astype(jnp.bfloat16)
    gsc[...] = gscore
    geno_t, trait_t = gscore.T, tscore.T

    def put(target, at, lhs, rhs):
        width = rhs.shape[1]
        target[:, :, :, at : at + width] = jnp.dot(lhs, rhs, preferred_element_type=F32).reshape(
            4, 8, 8, width
        )

    load.wait()
    running = []
    for (make, _, first, count, genos), part in zip(STREAMS, parts):
        for at in range(0, count, 256):
            put(part[0], at, trait_t, people_traits[:, first + at : first + at + 256])
        for at in range(0, genos, 256):
            put(part[0], count + at, geno_t, std[:, at : at + 256])
        running.append(make(net, *part))
        next(running[-1])
    together(running)
    scale = 1.0 / math.sqrt(people)
    for (_, _, first, count, genos), part in zip(STREAMS, parts):
        tl[:, first : first + count] = part[4][:, 0:count] * scale
        if genos:
            gl[...] = part[4][:, count : count + genos] * scale


def loadings(people, inv_own, cross_own, init, sketch, std, traits):
    vm = pl.BlockSpec(memory_space=pltpu.VMEM)
    sems = 5 + 2 * (6 + 7) + 2 * (14 + 3)
    return pl.pallas_call(
        functools.partial(loading_kernel, people),
        out_shape=[
            jax.ShapeDtypeStruct((640, 256), jnp.bfloat16),
            jax.ShapeDtypeStruct((640, 256), jnp.bfloat16),
            jax.ShapeDtypeStruct((8, 512), F32),
            jax.ShapeDtypeStruct((8, 4096), F32),
        ],
        in_specs=[vm] * 5 + [pl.BlockSpec(memory_space=pl.ANY)],
        out_specs=[vm] * 4,
        scratch_shapes=[
            pltpu.VMEM((2, 512, 512), F32),
            pltpu.VMEM((512, 512), F32),
            pltpu.VMEM((640, 4096), jnp.bfloat16),
            *[buffer for _, scratch, _, count, genos in STREAMS for buffer in scratch(count + genos)],
            pltpu.SemaphoreType.DMA((sems,)),
            pltpu.SemaphoreType.DMA((sems,)),
            pltpu.SemaphoreType.DMA,
        ],
        compiler_params=pltpu.CompilerParams(
            collective_id=2, has_side_effects=True, vmem_limit_bytes=56 << 20
        ),
        name="loadings",
    )(inv_own, cross_own, init, sketch, std, traits)


def on_device(genotypes, frequencies, traits, geno_sketch, trait_sketch, initial):
    people = genotypes.shape[0] * lax.axis_size("rows")
    shift = (2.0 * frequencies)[None, :]
    spread = lax.rsqrt(2.0 * frequencies * (1.0 - frequencies))[None, :]
    gram, cross, sketch, std = sketches(
        people, genotypes, shift, spread, traits, geno_sketch, trait_sketch
    )
    return tuple(loadings(people, inverse_factor(gram), cross, initial, sketch, std, traits))


def solution(mesh):
    placed = (
        P("rows", "cols"),
        P("cols"),
        P("rows", "cols"),
        P("cols", None),
        P("cols", None),
        P(),
    )
    return jax.shard_map(
        on_device,
        mesh=mesh,
        in_specs=placed,
        out_specs=(P("rows", None), P("rows", None), P("rows", "cols"), P("rows", "cols")),
        check_vma=False,
    )
```

```python
import functools
import math

import jax
import jax.numpy as jnp
from jax import lax
from jax.experimental import pallas as pl
from jax.experimental.pallas import tpu as pltpu
from jax.sharding import PartitionSpec as P

HI=lax.Precision.HIGHEST
F32=jnp.float32
def dotf(a,b,ca,cb):
    return lax.dot_general(a,b,(((ca,),(cb,)),((),())),precision=HI,preferred_element_type=F32)


def factor(d_ref):
    row = lax.broadcasted_iota(jnp.int32, (8, 128), 0)
    for p in range(16):
        rows = slice(8 * p, 8 * p + 8)
        gram, inverse = d_ref[rows, 0:128], d_ref[rows, 128:256]
        cell = {}
        for j in range(8):
            column = jnp.broadcast_to(gram[:, 8 * p + j : 8 * p + j + 1], (8, 128))
            for i in range(j, 8):
                cell[i, j] = column[i : i + 1, :]
        scales = []
        for j in range(8):
            scales.append(lax.rsqrt(cell[j, j]))
            if j == 7:
                break
            inv = 1.0 / cell[j, j]
            ratio = {i: cell[i, j] * inv for i in range(j + 1, 8)}
            for b in range(j + 1, 8):
                for i in range(b, 8):
                    cell[i, b] = cell[i, b] - ratio[i] * cell[b, j]
            factors = jnp.zeros((8, 128), F32)
            for i in range(j + 1, 8):
                factors = jnp.where(row == i, jnp.broadcast_to(ratio[i], (8, 128)), factors)
            inverse = inverse - factors * inverse[j : j + 1, :]
            gram = gram - factors * gram[j : j + 1, :]
        scale = jnp.broadcast_to(scales[0], (8, 128))
        for i in range(1, 8):
            scale = jnp.where(row == i, jnp.broadcast_to(scales[i], (8, 128)), scale)
        upper, under = gram * scale, inverse * scale
        d_ref[rows, 128:256] = under
        if p < 15:
            turned = upper.T
            for g in range(p + 1, 16):
                group = slice(8 * g, 8 * g + 8)
                left, right = d_ref[group, 0:128], d_ref[group, 128:256]
                for j in range(8):
                    times = turned[group, j : j + 1]
                    left = left - times * upper[j : j + 1, :]
                    right = right - times * under[j : j + 1, :]
                d_ref[group, 0:128] = left
                d_ref[group, 128:256] = right


MESH = pl.DeviceIdType.MESH


class Place:
    def __init__(self):
        rows, cols = lax.axis_index("rows"), lax.axis_index("cols")
        self.x, self.core = lax.div(cols, 2), lax.rem(cols, 2)
        self.y, self.z = lax.div(rows, 8), lax.rem(rows, 8)

    def ring(self, axis):
        return (self.z, 8) if axis == "z" else (getattr(self, axis), 4)

    def other(self, axis, step):
        here, size = self.ring(axis)
        return lax.rem(here + step + size, size)

    def device(self, axis, step):
        at = {"x": self.x, "y": self.y, "z": self.z, "core": self.core}
        at[axis] = 1 - self.core if axis == "core" else self.other(axis, step)
        return (at["y"] * 8 + at["z"], at["x"] * 2 + at["core"])


class Net:
    def __init__(self, place, sends, recvs):
        self.place, self.sends, self.recvs, self.count = place, sends, recvs, 0

    def greet(self, axes):
        barrier = pltpu.get_barrier_semaphore()
        partners = [(a, s) for a in axes for s in range(1, {"core": 2, "z": 8}.get(a, 4))]
        for axis, step in partners:
            pl.semaphore_signal(
                barrier, inc=1, device_id=self.place.device(axis, step), device_id_type=MESH
            )
        pl.semaphore_wait(barrier, len(partners))

    def send(self, source, target, axis, step=1):
        copy = self.plan(source, target, axis, step)
        copy.start()
        return copy

    def plan(self, source, target, axis, step=1):
        slot = self.count
        self.count += 1
        return pltpu.make_async_remote_copy(
            src_ref=source,
            dst_ref=target,
            send_sem=self.sends.at[slot],
            recv_sem=self.recvs.at[slot],
            device_id=self.place.device(axis, step),
            device_id_type=MESH,
        )

    def scatter(self, axis, part, landing):
        size = self.place.ring(axis)[1]
        order = sorted(range(1, size), key=lambda s: -min(s, size - s))
        return [
            self.send(part(self.place.other(axis, s)), landing.at[s - 1], axis, s) for s in order
        ]

    def gather(self, axis, own):
        size = self.place.ring(axis)[1]
        order = sorted(range(1, size), key=lambda s: -min(s, size - s))
        return [self.send(own, own, axis, s) for s in order]


def ring_scatter(net, axis, part, lands):
    place = net.place
    size = place.ring(axis)[1]
    turns = size // 2
    ways = ((0, 1), (1, size - 1))
    flight = {d: {d: net.send(part(place.other(axis, turns), d), lands(d, 0, d), axis, s)} for d, s in ways}
    sent = [flight[d][d] for d, _ in ways]
    for hop in range(1, turns):
        leaving = {0: {}, 1: {}}
        if hop == 1:
            for d, s in ways:
                chunk = place.other(axis, turns - 1 if d == 0 else 1 - turns)
                leaving[d][1 - d] = net.send(part(chunk, 1 - d), lands(d, 1, 1 - d), axis, s)
        yield
        for first in (True, False):
            for d, s in ways:
                h = d if first else 1 - d
                if h not in flight[d]:
                    continue
                chunk = place.other(axis, turns - hop if d == 0 else hop - turns)
                flight[d][h].wait_recv()
                passed, mine = lands(d, hop - 1, h), part(chunk, h)
                passed[...] = passed[...] + mine[...]
                leaving[d][h] = net.send(passed, lands(d, hop, h), axis, s)
        flight = leaving
        sent += [flight[d][h] for d in (0, 1) for h in (0, 1)]
    yield
    for d, _ in ways:
        for h in (0, 1):
            flight[d][h].wait_recv()
    for copy in sent:
        copy.wait_send()


def finish(copies):
    for copy in copies:
        copy.wait()


def rows_of(index, count):
    return pl.ds(pl.multiple_of(index * count, count), count)


def total_of(landing):
    total = landing[0]
    for s in range(1, landing.shape[0]):
        total = total + landing[s]
    return total


def gram_stream(net, axes, source, land1, part1, land2, part2, land3, out3, out2, out1):
    place = net.place
    first, second = axes
    i1, i2, z = place.ring(first)[0], place.ring(second)[0], place.z
    copies = net.scatter(first, lambda i: source.at[rows_of(i, 288)], land1)
    yield
    finish(copies)
    part1[...] = source[rows_of(i1, 288)] + total_of(land1)
    copies = net.scatter(second, lambda i: part1.at[rows_of(i, 72)], land2)
    part2[72:128] = jnp.zeros((56, 128), F32)
    yield
    finish(copies)
    part2[0:72] = part1[rows_of(i2, 72)] + total_of(land2)
    copies = net.scatter("z", lambda i: part2.at[rows_of(i, 16)], land3)
    yield
    finish(copies)
    out3[rows_of(z, 16)] = part2[rows_of(z, 16)] + total_of(land3)
    copies = net.gather("z", out3.at[rows_of(z, 16)])
    yield
    finish(copies)
    out2[i2] = out3[0:72]
    copies = net.gather(second, out2.at[i2])
    yield
    finish(copies)
    out1[i1] = out2[...]
    copies = net.gather(first, out1.at[i1])
    yield
    finish(copies)


GRAM_SCRATCH = [
    pltpu.VMEM((3, 288, 128), F32),
    pltpu.VMEM((288, 128), F32),
    pltpu.VMEM((3, 72, 128), F32),
    pltpu.VMEM((128, 128), F32),
    pltpu.VMEM((7, 16, 128), F32),
    pltpu.VMEM((128, 128), F32),
    pltpu.VMEM((4, 72, 128), F32),
    pltpu.VMEM((4, 4, 72, 128), F32),
]
UPPER = [(i, j) for j in range(4) for i in range(j + 1)]


def together(streams):
    streams = list(streams)
    while streams:
        alive = []
        for stream in streams:
            try:
                next(stream)
                alive.append(stream)
            except StopIteration:
                pass
        streams = alive


def unit(v):
    return v * lax.rsqrt(jnp.mean(v * v, axis=0, keepdims=True) + 1e-06)


def rows_first(net, source, land1, part1, land2, out):
    place, half = net.place, source.shape[-1] // 2
    yield from ring_scatter(
        net,
        "y",
        lambda i, h: source.at[i, :, :, half * h : half * h + half],
        lambda d, hop, h: land1.at[d, hop, :, :, half * h : half * h + half],
    )
    part1[...] = source[place.y] + land1[0, 1] + land1[1, 1]
    copies = net.scatter("z", lambda i: part1.at[i], land2)
    yield
    finish(copies)
    out[...] = part1[place.z] + total_of(land2)


def ring_first(net, source, land1, part1, land2, out):
    place, half = net.place, source.shape[-1] // 2
    yield from ring_scatter(
        net,
        "z",
        lambda i, h: source.at[:, i, :, half * h : half * h + half],
        lambda d, hop, h: land1.at[d, hop, :, :, half * h : half * h + half],
    )
    part1[...] = source[:, place.z] + land1[0, 3] + land1[1, 3]
    copies = net.scatter("y", lambda i: part1.at[i], land2)
    yield
    finish(copies)
    out[...] = part1[place.y] + total_of(land2)


def rows_scratch(width):
    return [
        pltpu.VMEM((4, 8, 8, width), F32),
        pltpu.VMEM((2, 2, 8, 8, width), F32),
        pltpu.VMEM((8, 8, width), F32),
        pltpu.VMEM((7, 8, width), F32),
        pltpu.VMEM((8, width), F32),
    ]


def ring_scratch(width):
    return [
        pltpu.VMEM((4, 8, 8, width), F32),
        pltpu.VMEM((2, 4, 4, 8, width), F32),
        pltpu.VMEM((4, 8, width), F32),
        pltpu.VMEM((3, 8, width), F32),
        pltpu.VMEM((8, width), F32),
    ]


STREAMS = (
    (rows_first, rows_scratch, 0, 1024, 0),
    (ring_first, ring_scratch, 1024, 1024, 0),
    (ring_first, ring_scratch, 2048, 256, 512),
    (rows_first, rows_scratch, 2304, 1024, 0),
    (rows_first, rows_scratch, 3328, 768, 0),
)
TURNS = (0, 1, 2, 1, 0, 3, 2, 1, 0, 2, 4, 3, 1, 2, 3, 0, 4, 1, 2, 3, 4, 1, 2, 3, 4)


def invert(a_ref, d_ref, done):
    eye = (
        lax.broadcasted_iota(jnp.int32, (128, 128), 0) == lax.broadcasted_iota(jnp.int32, (128, 128), 1)
    ).astype(F32)
    a_ref[:, 512:1024] = jnp.zeros((512, 512), F32)
    for k in range(4):
        a_ref[128 * k : 128 * k + 128, 512 + 128 * k : 640 + 128 * k] = eye

    def body(k, _):
        for kk in range(4):

            @pl.when(k == kk)
            def _():
                d_ref[:, 0:128] = a_ref[128 * kk : 128 * kk + 128, 128 * kk : 128 * kk + 128]
                d_ref[:, 128:256] = eye

        factor(d_ref)
        for kk in range(4):

            @pl.when(k == kk)
            def _():
                lo = 128 * (kk + 1)
                block = slice(128 * kk, 128 * kk + 128)
                panel = dotf(d_ref[:, 128:256], a_ref[block, lo : lo + 512], 1, 0)
                a_ref[block, lo : lo + 512] = panel
                done(kk)
                if kk < 3:
                    a_ref[lo:512, lo : lo + 512] = a_ref[lo:512, lo : lo + 512] - dotf(
                        panel[:, : 512 - lo].T, panel, 1, 0
                    )

        return 0

    lax.fori_loop(0, 4, body, 0)


def cca_kernel(people, geno_in, freq, traits_in, gsk_in, tsk_in, init, scores, loads, *scratch):
    geno, traits, gsk, tsk, std, give, take, held, lands, both, source = scratch[:11]
    alpha, beta = scratch[11:19], scratch[19:27]
    a_ref, d_ref, inv, cross, full = scratch[27:32]
    parts = [scratch[32 + 5 * s : 37 + 5 * s] for s in range(5)]
    sends, recvs, loaded = scratch[57:60]
    place = Place()
    net = Net(place, sends, recvs)
    x, k = place.x, place.core
    cols = pl.ds(pl.multiple_of(256 * k, 256), 256)

    def load(slot, origin, target):
        copy = pltpu.make_async_copy(origin, target, loaded.at[slot])
        copy.start()
        return copy

    def half_load(slot, half):
        rows = rows_of(half, 320)
        return load(slot, traits_in.at[rows], traits.at[rows])

    loads_of = [
        load(0, tsk_in.at[:, 0:256], tsk.at[:, 0:256]),
        half_load(1, 1 - k),
        load(2, geno_in, geno),
        load(3, tsk_in.at[:, 256:512], tsk.at[:, 256:512]),
        load(4, gsk_in, gsk),
        half_load(5, k),
    ]
    net.greet(("core", "x", "y", "z"))

    def piece(half, j):
        rows = rows_of(half, 320)
        if j < 2:
            return jnp.dot(traits[rows], tsk[:, 256 * j : 256 * j + 256], preferred_element_type=F32)
        j -= 2
        return jnp.dot(std[rows], gsk[:, 256 * j : 256 * j + 256], preferred_element_type=F32)

    copies = []
    finish(loads_of[:2])
    for j in range(4):
        if j == 1:
            loads_of[3].wait()
        if j == 2:
            finish([loads_of[2], loads_of[4]])
            spread = lax.rsqrt(2.0 * freq[...] * (1.0 - freq[...]))
            std[...] = ((geno[...].astype(F32) - 2.0 * freq[...]) * spread).astype(jnp.bfloat16)
        give[j] = piece(1 - k, j)
        copies.append(net.send(give.at[j], take.at[j], "core"))
    loads_of[5].wait()

    def part(j, step):
        return held.at[j, rows_of(place.other("x", step), 80)]

    far, near = [], []
    for j in range(4):
        mine = piece(k, j)
        copies[j].wait()
        held[j] = mine + take[j]
        toward, away = (1, 3) if j < 2 else (3, 1)
        far.append(net.send(part(j, 2), lands.at[0, j], "x", toward))
        near.append(net.send(part(j, away), lands.at[1, j], "x", away))
    passing = []
    for j in range(4):
        toward = 1 if j < 2 else 3
        far[j].wait_recv()
        lands[0, j] = lands[0, j] + part(j, toward)[...]
        passing.append(net.send(lands.at[0, j], lands.at[2, j], "x", toward))
    for j in range(4):
        near[j].wait_recv()
        passing[j].wait_recv()
        at = 512 + 256 * j if j < 2 else 256 * j - 512
        both[k, :, at : at + 256] = part(j, 0)[...] + lands[1, j] + lands[2, j]
    copy = net.send(both.at[k], both.at[k], "core")
    for other in far + near + passing:
        other.wait_send()
    copy.wait()
    flat = both[...].reshape(160, 1024)
    view = both[:, :, pl.ds(pl.multiple_of(512 * k, 512), 512)].reshape(160, 512)
    side = both[:, :, pl.ds(pl.multiple_of(512 + 256 * k, 256), 256)].reshape(160, 256)
    gram = dotf(view.T, view, 1, 0)
    for t, (i, j) in enumerate(UPPER):
        source[128 * t : 128 * t + 128] = gram[128 * i : 128 * i + 128, 128 * j : 128 * j + 128]
    crossed = dotf(flat[:, 0:512].T, side, 1, 0)
    for j in range(2):
        for i in range(4):
            t = 10 + 4 * j + i
            source[128 * t : 128 * t + 128] = crossed[128 * i : 128 * i + 128, 128 * j : 128 * j + 128]
    together(
        [
            gram_stream(net, ("x", "y"), source.at[0:1152], *alpha),
            gram_stream(net, ("y", "x"), source.at[1152:2304], *beta),
        ]
    )
    for s, stream in enumerate((alpha, beta)):
        for i in range(4):
            for j in range(4):
                at = 1152 * s + 288 * i + 72 * j
                source[at : at + 72] = stream[7][i, j]

    full[k * 4 + x] = both[k]
    full[(1 - k) * 4 + x] = both[1 - k]
    here = full.at[k * 4 + x]
    across = [net.send(here, here, "x", s) for s in (2, 1, 3)]
    scale = 1.0 / people
    a_ref[:, 0:512] = jnp.zeros((512, 512), F32)
    for t, (i, j) in enumerate(UPPER):
        a_ref[128 * i : 128 * i + 128, 128 * j : 128 * j + 128] = source[128 * t : 128 * t + 128] * scale
    for j in range(2):
        at = pl.ds(pl.multiple_of(256 * k + 128 * j, 128), 128)
        for i in range(4):
            t = 10 + 4 * j + i
            cross[128 * i : 128 * i + 128, at] = source[128 * t : 128 * t + 128] * scale
    pair = [net.send(cross.at[:, cols], cross.at[:, cols], "core")]
    swaps = []
    for i in range(4):
        block = (slice(128 * i, 128 * i + 128), slice(0, 128 * i + 128))
        swaps.append(net.plan(inv.at[(k, *block)], inv.at[(k, *block)], "core"))
        if i < 3:
            rest = slice(128 * i + 128, 512)
            for v in range(2):
                inv[v, 128 * i : 128 * i + 128, rest] = jnp.zeros((128, 384 - 128 * i), F32)

    def done(i):
        block = (slice(128 * i, 128 * i + 128), slice(0, 128 * i + 128))
        inv[(k, *block)] = a_ref[128 * i : 128 * i + 128, 512 : 640 + 128 * i]
        swaps[i].start()

    invert(a_ref, d_ref, done)
    for s, copy in zip((2, 1, 3), across):
        copy.wait()
        came = full.at[k * 4 + place.other("x", -s)]
        pair.append(net.send(came, came, "core"))
    finish(swaps)
    pair[0].wait()
    left = unit(dotf(inv[0], dotf(cross[...], dotf(inv[1], init[...], 0, 0), 1, 0), 1, 0))
    scale = 1.0 / math.sqrt(inv.shape[1])
    geno_weights = dotf(inv[0], left, 0, 0)
    right = unit(dotf(inv[1], dotf(cross[...], geno_weights, 0, 0), 1, 0))
    trait_weights = dotf(inv[1], right, 0, 0)
    finish(pair[1:])
    flat = full[...].reshape(640, 1024)
    tscore = dotf(flat[:, 512:1024], trait_weights * scale, 1, 0).astype(jnp.bfloat16)
    trait_t = tscore.T

    def put(target, at, lhs, rhs):
        width = rhs.shape[1]
        target[:, :, :, at : at + width] = jnp.dot(lhs, rhs, preferred_element_type=F32).reshape(
            4, 8, 8, width
        )

    scores[:, 256:512] = tscore
    running = {}
    geno_t = None
    for turn in TURNS:
        if turn not in running:
            make, _, first, count, genos = STREAMS[turn]
            target = parts[turn][0]
            for at in range(0, count, 256):
                put(target, at, trait_t, traits[:, first + at : first + at + 256])
            if genos:
                gscore = dotf(flat[:, 0:512], geno_weights * scale, 1, 0).astype(jnp.bfloat16)
                scores[:, 0:256] = gscore
                geno_t = gscore.T
            for at in range(0, genos, 256):
                put(target, count + at, geno_t, std[:, at : at + 256])
            running[turn] = make(net, *parts[turn])
        next(running[turn], None)
    together(running.values())
    scale = 1.0 / math.sqrt(people)
    for (_, _, first, count, genos), part_of in zip(STREAMS, parts):
        loads[:, 512 + first : 512 + first + count] = part_of[4][:, 0:count] * scale
        if genos:
            loads[:, 0:512] = part_of[4][:, count : count + genos] * scale


def cca(people, geno, freq, traits, gsk, tsk, init):
    vm, far = pl.BlockSpec(memory_space=pltpu.VMEM), pl.BlockSpec(memory_space=pl.ANY)
    sems = 4 + 12 + 1 + 2 * (2 * (3 + 3 + 7)) + 3 + 1 + 4 + 3 + 3 * (6 + 7) + 2 * (14 + 3)
    return pl.pallas_call(
        functools.partial(cca_kernel, people),
        out_shape=[
            jax.ShapeDtypeStruct((640, 512), jnp.bfloat16),
            jax.ShapeDtypeStruct((8, 4608), F32),
        ],
        in_specs=[far, vm, far, far, far, vm],
        out_specs=[vm] * 2,
        scratch_shapes=[
            pltpu.VMEM((640, 512), jnp.int32),
            pltpu.VMEM((640, 4096), jnp.bfloat16),
            pltpu.VMEM((512, 512), jnp.bfloat16),
            pltpu.VMEM((4096, 512), jnp.bfloat16),
            pltpu.VMEM((640, 512), jnp.bfloat16),
            pltpu.VMEM((4, 320, 256), F32),
            pltpu.VMEM((4, 320, 256), F32),
            pltpu.VMEM((4, 320, 256), F32),
            pltpu.VMEM((3, 4, 80, 256), F32),
            pltpu.VMEM((2, 80, 1024), F32),
            pltpu.VMEM((2304, 128), F32),
            *GRAM_SCRATCH,
            *GRAM_SCRATCH,
            pltpu.VMEM((512, 1024), F32),
            pltpu.VMEM((128, 256), F32),
            pltpu.VMEM((2, 512, 512), F32),
            pltpu.VMEM((512, 512), F32),
            pltpu.VMEM((8, 80, 1024), F32),
            *[buffer for _, scratch, _, count, genos in STREAMS for buffer in scratch(count + genos)],
            pltpu.SemaphoreType.DMA((sems,)),
            pltpu.SemaphoreType.DMA((sems,)),
            pltpu.SemaphoreType.DMA((6,)),
        ],
        compiler_params=pltpu.CompilerParams(
            collective_id=1, has_side_effects=True, vmem_limit_bytes=60 << 20
        ),
        name="cca",
    )(geno, freq, traits, gsk, tsk, init)


def on_device(genotypes, frequencies, traits, geno_sketch, trait_sketch, initial):
    people = genotypes.shape[0] * lax.axis_size("rows")
    scores, loads = cca(
        people, genotypes, frequencies[None, :], traits, geno_sketch, trait_sketch, initial
    )
    pairs, width = initial.shape[1], genotypes.shape[1]
    return (scores[:, :pairs], scores[:, pairs:], loads[:, :width], loads[:, width:])


def solution(mesh):
    placed = (
        P("rows", "cols"),
        P("cols"),
        P("rows", "cols"),
        P("cols", None),
        P("cols", None),
        P(),
    )
    return jax.shard_map(
        on_device,
        mesh=mesh,
        in_specs=placed,
        out_specs=(P("rows", None), P("rows", None), P("rows", "cols"), P("rows", "cols")),
        check_vma=False,
    )
```

```python
import functools
import math

import jax
import jax.numpy as jnp
from jax import lax
from jax.experimental import pallas as pl
from jax.experimental.pallas import tpu as pltpu
from jax.sharding import PartitionSpec as P

HI=lax.Precision.HIGHEST
F32=jnp.float32
def dotf(a,b,ca,cb):
    return lax.dot_general(a,b,(((ca,),(cb,)),((),())),precision=HI,preferred_element_type=F32)


def factor(d_ref):
    row = lax.broadcasted_iota(jnp.int32, (8, 128), 0)
    for p in range(16):
        rows = slice(8 * p, 8 * p + 8)
        gram, inverse = d_ref[rows, 0:128], d_ref[rows, 128:256]
        cell = {}
        for j in range(8):
            column = jnp.broadcast_to(gram[:, 8 * p + j : 8 * p + j + 1], (8, 128))
            for i in range(j, 8):
                cell[i, j] = column[i : i + 1, :]
        scales = []
        for j in range(8):
            scales.append(lax.rsqrt(cell[j, j]))
            if j == 7:
                break
            inv = 1.0 / cell[j, j]
            ratio = {i: cell[i, j] * inv for i in range(j + 1, 8)}
            for b in range(j + 1, 8):
                for i in range(b, 8):
                    cell[i, b] = cell[i, b] - ratio[i] * cell[b, j]
            factors = jnp.zeros((8, 128), F32)
            for i in range(j + 1, 8):
                factors = jnp.where(row == i, jnp.broadcast_to(ratio[i], (8, 128)), factors)
            inverse = inverse - factors * inverse[j : j + 1, :]
            gram = gram - factors * gram[j : j + 1, :]
        scale = jnp.broadcast_to(scales[0], (8, 128))
        for i in range(1, 8):
            scale = jnp.where(row == i, jnp.broadcast_to(scales[i], (8, 128)), scale)
        upper, under = gram * scale, inverse * scale
        d_ref[rows, 128:256] = under
        if p < 15:
            turned = upper.T
            for g in range(p + 1, 16):
                group = slice(8 * g, 8 * g + 8)
                left, right = d_ref[group, 0:128], d_ref[group, 128:256]
                for j in range(8):
                    times = turned[group, j : j + 1]
                    left = left - times * upper[j : j + 1, :]
                    right = right - times * under[j : j + 1, :]
                d_ref[group, 0:128] = left
                d_ref[group, 128:256] = right


MESH = pl.DeviceIdType.MESH


class Place:
    def __init__(self):
        rows, cols = lax.axis_index("rows"), lax.axis_index("cols")
        self.x, self.core = lax.div(cols, 2), lax.rem(cols, 2)
        self.y, self.z = lax.div(rows, 8), lax.rem(rows, 8)

    def ring(self, axis):
        return (self.z, 8) if axis == "z" else (getattr(self, axis), 4)

    def other(self, axis, step):
        here, size = self.ring(axis)
        return lax.rem(here + step + size, size)

    def device(self, axis, step):
        at = {"x": self.x, "y": self.y, "z": self.z, "core": self.core}
        at[axis] = 1 - self.core if axis == "core" else self.other(axis, step)
        return (at["y"] * 8 + at["z"], at["x"] * 2 + at["core"])


class Net:
    def __init__(self, place, sends, recvs):
        self.place, self.sends, self.recvs, self.count = place, sends, recvs, 0

    def greet(self, axes):
        barrier = pltpu.get_barrier_semaphore()
        partners = [(a, s) for a in axes for s in range(1, {"core": 2, "z": 8}.get(a, 4))]
        for axis, step in partners:
            pl.semaphore_signal(
                barrier, inc=1, device_id=self.place.device(axis, step), device_id_type=MESH
            )
        pl.semaphore_wait(barrier, len(partners))

    def send(self, source, target, axis, step=1):
        copy = self.plan(source, target, axis, step)
        copy.start()
        return copy

    def plan(self, source, target, axis, step=1):
        slot = self.count
        self.count += 1
        return pltpu.make_async_remote_copy(
            src_ref=source,
            dst_ref=target,
            send_sem=self.sends.at[slot],
            recv_sem=self.recvs.at[slot],
            device_id=self.place.device(axis, step),
            device_id_type=MESH,
        )

    def scatter(self, axis, part, landing):
        size = self.place.ring(axis)[1]
        order = sorted(range(1, size), key=lambda s: -min(s, size - s))
        return [
            self.send(part(self.place.other(axis, s)), landing.at[s - 1], axis, s) for s in order
        ]

    def gather(self, axis, own):
        size = self.place.ring(axis)[1]
        order = sorted(range(1, size), key=lambda s: -min(s, size - s))
        return [self.send(own, own, axis, s) for s in order]


def ring_scatter(net, axis, part, lands):
    place = net.place
    size = place.ring(axis)[1]
    turns = size // 2
    ways = ((0, 1), (1, size - 1))
    flight = {d: {d: net.send(part(place.other(axis, turns), d), lands(d, 0, d), axis, s)} for d, s in ways}
    sent = [flight[d][d] for d, _ in ways]
    for hop in range(1, turns):
        leaving = {0: {}, 1: {}}
        if hop == 1:
            for d, s in ways:
                chunk = place.other(axis, turns - 1 if d == 0 else 1 - turns)
                leaving[d][1 - d] = net.send(part(chunk, 1 - d), lands(d, 1, 1 - d), axis, s)
        yield
        for first in (True, False):
            for d, s in ways:
                h = d if first else 1 - d
                if h not in flight[d]:
                    continue
                chunk = place.other(axis, turns - hop if d == 0 else hop - turns)
                flight[d][h].wait_recv()
                passed, mine = lands(d, hop - 1, h), part(chunk, h)
                passed[...] = passed[...] + mine[...]
                leaving[d][h] = net.send(passed, lands(d, hop, h), axis, s)
        flight = leaving
        sent += [flight[d][h] for d in (0, 1) for h in (0, 1)]
    yield
    for d, _ in ways:
        for h in (0, 1):
            flight[d][h].wait_recv()
    for copy in sent:
        copy.wait_send()


def finish(copies):
    for copy in copies:
        copy.wait()


def rows_of(index, count):
    return pl.ds(pl.multiple_of(index * count, count), count)


def total_of(landing):
    total = landing[0]
    for s in range(1, landing.shape[0]):
        total = total + landing[s]
    return total


def gram_stream(net, axes, source, land1, part1, land2, part2, land3, out3, out2, out1):
    place = net.place
    first, second = axes
    i1, i2, z = place.ring(first)[0], place.ring(second)[0], place.z
    copies = net.scatter(first, lambda i: source.at[rows_of(i, 288)], land1)
    yield
    finish(copies)
    part1[...] = source[rows_of(i1, 288)] + total_of(land1)
    copies = net.scatter(second, lambda i: part1.at[rows_of(i, 72)], land2)
    part2[72:128] = jnp.zeros((56, 128), F32)
    yield
    finish(copies)
    part2[0:72] = part1[rows_of(i2, 72)] + total_of(land2)
    copies = net.scatter("z", lambda i: part2.at[rows_of(i, 16)], land3)
    yield
    finish(copies)
    out3[rows_of(z, 16)] = part2[rows_of(z, 16)] + total_of(land3)
    copies = net.gather("z", out3.at[rows_of(z, 16)])
    yield
    finish(copies)
    out2[i2] = out3[0:72]
    copies = net.gather(second, out2.at[i2])
    yield
    finish(copies)
    out1[i1] = out2[...]
    copies = net.gather(first, out1.at[i1])
    yield
    finish(copies)


GRAM_SCRATCH = [
    pltpu.VMEM((3, 288, 128), F32),
    pltpu.VMEM((288, 128), F32),
    pltpu.VMEM((3, 72, 128), F32),
    pltpu.VMEM((128, 128), F32),
    pltpu.VMEM((7, 16, 128), F32),
    pltpu.VMEM((128, 128), F32),
    pltpu.VMEM((4, 72, 128), F32),
    pltpu.VMEM((4, 4, 72, 128), F32),
]
UPPER = [(i, j) for j in range(4) for i in range(j + 1)]


def together(streams):
    streams = list(streams)
    while streams:
        alive = []
        for stream in streams:
            try:
                next(stream)
                alive.append(stream)
            except StopIteration:
                pass
        streams = alive


def unit(v):
    return v * lax.rsqrt(jnp.mean(v * v, axis=0, keepdims=True) + 1e-06)


def rows_first(net, source, land1, part1, land2, out):
    place, half = net.place, source.shape[-1] // 2
    yield from ring_scatter(
        net,
        "y",
        lambda i, h: source.at[i, :, :, half * h : half * h + half],
        lambda d, hop, h: land1.at[d, hop, :, :, half * h : half * h + half],
    )
    part1[...] = source[place.y] + land1[0, 1] + land1[1, 1]
    copies = net.scatter("z", lambda i: part1.at[i], land2)
    yield
    finish(copies)
    out[...] = part1[place.z] + total_of(land2)


def rings_only(net, source, land1, part1, land2, out):
    place, half = net.place, source.shape[-1] // 2
    yield from ring_scatter(
        net,
        "y",
        lambda i, h: source.at[i, :, :, half * h : half * h + half],
        lambda d, hop, h: land1.at[d, hop, :, :, half * h : half * h + half],
    )
    part1[...] = source[place.y] + land1[0, 1] + land1[1, 1]
    yield from ring_scatter(
        net,
        "z",
        lambda i, h: part1.at[i, :, half * h : half * h + half],
        lambda d, hop, h: land2.at[d, hop, :, half * h : half * h + half],
    )
    out[...] = part1[place.z] + land2[0, 3] + land2[1, 3]


def ring_first(net, source, land1, part1, land2, out):
    place, half = net.place, source.shape[-1] // 2
    yield from ring_scatter(
        net,
        "z",
        lambda i, h: source.at[:, i, :, half * h : half * h + half],
        lambda d, hop, h: land1.at[d, hop, :, :, half * h : half * h + half],
    )
    part1[...] = source[:, place.z] + land1[0, 3] + land1[1, 3]
    copies = net.scatter("y", lambda i: part1.at[i], land2)
    yield
    finish(copies)
    out[...] = part1[place.y] + total_of(land2)


def rows_scratch(width):
    return [
        pltpu.VMEM((4, 8, 8, width), F32),
        pltpu.VMEM((2, 2, 8, 8, width), F32),
        pltpu.VMEM((8, 8, width), F32),
        pltpu.VMEM((7, 8, width), F32),
        pltpu.VMEM((8, width), F32),
    ]


def rings_scratch(width):
    return [
        pltpu.VMEM((4, 8, 8, width), F32),
        pltpu.VMEM((2, 2, 8, 8, width), F32),
        pltpu.VMEM((8, 8, width), F32),
        pltpu.VMEM((2, 4, 8, width), F32),
        pltpu.VMEM((8, width), F32),
    ]


def ring_scratch(width):
    return [
        pltpu.VMEM((4, 8, 8, width), F32),
        pltpu.VMEM((2, 4, 4, 8, width), F32),
        pltpu.VMEM((4, 8, width), F32),
        pltpu.VMEM((3, 8, width), F32),
        pltpu.VMEM((8, width), F32),
    ]


STREAMS = (
    (rings_only, rings_scratch, 0, 1536, 0),
    (ring_first, ring_scratch, 1536, 1024, 0),
    (ring_first, ring_scratch, 2560, 512, 512),
    (rows_first, rows_scratch, 3072, 1024, 0),
)
TURNS = (0, 1, 2, 1, 0, 3, 2, 1, 2, 0, 3, 1, 2, 0, 3)


def invert(a_ref, d_ref, done):
    eye = (
        lax.broadcasted_iota(jnp.int32, (128, 128), 0) == lax.broadcasted_iota(jnp.int32, (128, 128), 1)
    ).astype(F32)
    a_ref[:, 512:1024] = jnp.zeros((512, 512), F32)
    for k in range(4):
        a_ref[128 * k : 128 * k + 128, 512 + 128 * k : 640 + 128 * k] = eye

    def body(k, _):
        for kk in range(4):

            @pl.when(k == kk)
            def _():
                d_ref[:, 0:128] = a_ref[128 * kk : 128 * kk + 128, 128 * kk : 128 * kk + 128]
                d_ref[:, 128:256] = eye

        factor(d_ref)
        for kk in range(4):

            @pl.when(k == kk)
            def _():
                lo = 128 * (kk + 1)
                block = slice(128 * kk, 128 * kk + 128)
                panel = dotf(d_ref[:, 128:256], a_ref[block, lo : lo + 512], 1, 0)
                a_ref[block, lo : lo + 512] = panel
                done(kk)
                if kk < 3:
                    a_ref[lo:512, lo : lo + 512] = a_ref[lo:512, lo : lo + 512] - dotf(
                        panel[:, : 512 - lo].T, panel, 1, 0
                    )

        return 0

    lax.fori_loop(0, 4, body, 0)


def cca_kernel(people, geno_in, freq, traits_in, gsk_in, tsk_in, init, scores, loads, *scratch):
    geno, traits, gsk, tsk, std, give, take, held, lands, both, source = scratch[:11]
    alpha, beta = scratch[11:19], scratch[19:27]
    a_ref, d_ref, inv, cross, full = scratch[27:32]
    parts = [scratch[32 + 5 * s : 37 + 5 * s] for s in range(4)]
    sends, recvs, loaded = scratch[52:55]
    place = Place()
    net = Net(place, sends, recvs)
    x, k = place.x, place.core
    cols = pl.ds(pl.multiple_of(256 * k, 256), 256)

    def load(slot, origin, target):
        copy = pltpu.make_async_copy(origin, target, loaded.at[slot])
        copy.start()
        return copy

    def half_load(slot, half):
        rows = rows_of(half, 320)
        return load(slot, traits_in.at[rows], traits.at[rows])

    loads_of = [
        load(0, tsk_in.at[:, 0:256], tsk.at[:, 0:256]),
        half_load(1, 1 - k),
        load(2, geno_in, geno),
        load(3, tsk_in.at[:, 256:512], tsk.at[:, 256:512]),
        load(4, gsk_in, gsk),
        half_load(5, k),
    ]
    net.greet(("core", "x", "y", "z"))

    def piece(half, j):
        rows = rows_of(half, 320)
        if j < 2:
            return jnp.dot(traits[rows], tsk[:, 256 * j : 256 * j + 256], preferred_element_type=F32)
        j -= 2
        return jnp.dot(std[rows], gsk[:, 256 * j : 256 * j + 256], preferred_element_type=F32)

    copies = []
    finish(loads_of[:2])
    for j in range(4):
        if j == 1:
            loads_of[3].wait()
        if j == 2:
            finish([loads_of[2], loads_of[4]])
            spread = lax.rsqrt(2.0 * freq[...] * (1.0 - freq[...]))
            std[...] = ((geno[...].astype(F32) - 2.0 * freq[...]) * spread).astype(jnp.bfloat16)
        give[j] = piece(1 - k, j)
        copies.append(net.send(give.at[j], take.at[j], "core"))
    loads_of[5].wait()

    def part(j, step):
        return held.at[j, rows_of(place.other("x", step), 80)]

    far, near = [], []
    for j in range(4):
        mine = piece(k, j)
        copies[j].wait()
        held[j] = mine + take[j]
        toward, away = (1, 3) if j < 2 else (3, 1)
        far.append(net.send(part(j, 2), lands.at[0, j], "x", toward))
        near.append(net.send(part(j, away), lands.at[1, j], "x", away))
    passing = []
    for j in range(4):
        toward = 1 if j < 2 else 3
        far[j].wait_recv()
        lands[0, j] = lands[0, j] + part(j, toward)[...]
        passing.append(net.send(lands.at[0, j], lands.at[2, j], "x", toward))
    for j in range(4):
        near[j].wait_recv()
        passing[j].wait_recv()
        at = 512 + 256 * j if j < 2 else 256 * j - 512
        both[k, :, at : at + 256] = part(j, 0)[...] + lands[1, j] + lands[2, j]
    copy = net.send(both.at[k], both.at[k], "core")
    for other in far + near + passing:
        other.wait_send()
    copy.wait()
    flat = both[...].reshape(160, 1024)
    view = both[:, :, pl.ds(pl.multiple_of(512 * k, 512), 512)].reshape(160, 512)
    side = both[:, :, pl.ds(pl.multiple_of(512 + 256 * k, 256), 256)].reshape(160, 256)
    gram = dotf(view.T, view, 1, 0)
    for t, (i, j) in enumerate(UPPER):
        source[128 * t : 128 * t + 128] = gram[128 * i : 128 * i + 128, 128 * j : 128 * j + 128]
    crossed = dotf(flat[:, 0:512].T, side, 1, 0)
    for j in range(2):
        for i in range(4):
            t = 10 + 4 * j + i
            source[128 * t : 128 * t + 128] = crossed[128 * i : 128 * i + 128, 128 * j : 128 * j + 128]
    together(
        [
            gram_stream(net, ("x", "y"), source.at[0:1152], *alpha),
            gram_stream(net, ("y", "x"), source.at[1152:2304], *beta),
        ]
    )
    for s, stream in enumerate((alpha, beta)):
        for i in range(4):
            for j in range(4):
                at = 1152 * s + 288 * i + 72 * j
                source[at : at + 72] = stream[7][i, j]

    full[k * 4 + x] = both[k]
    full[(1 - k) * 4 + x] = both[1 - k]
    here = full.at[k * 4 + x]
    across = [net.send(here, here, "x", s) for s in (2, 1, 3)]
    scale = 1.0 / people
    a_ref[:, 0:512] = jnp.zeros((512, 512), F32)
    for t, (i, j) in enumerate(UPPER):
        a_ref[128 * i : 128 * i + 128, 128 * j : 128 * j + 128] = source[128 * t : 128 * t + 128] * scale
    for j in range(2):
        at = pl.ds(pl.multiple_of(256 * k + 128 * j, 128), 128)
        for i in range(4):
            t = 10 + 4 * j + i
            cross[128 * i : 128 * i + 128, at] = source[128 * t : 128 * t + 128] * scale
    pair = [net.send(cross.at[:, cols], cross.at[:, cols], "core")]
    swaps = []
    for i in range(4):
        block = (slice(128 * i, 128 * i + 128), slice(0, 128 * i + 128))
        swaps.append(net.plan(inv.at[(k, *block)], inv.at[(k, *block)], "core"))
        if i < 3:
            rest = slice(128 * i + 128, 512)
            for v in range(2):
                inv[v, 128 * i : 128 * i + 128, rest] = jnp.zeros((128, 384 - 128 * i), F32)

    def done(i):
        block = (slice(128 * i, 128 * i + 128), slice(0, 128 * i + 128))
        inv[(k, *block)] = a_ref[128 * i : 128 * i + 128, 512 : 640 + 128 * i]
        swaps[i].start()

    invert(a_ref, d_ref, done)
    for s, copy in zip((2, 1, 3), across):
        copy.wait()
        came = full.at[k * 4 + place.other("x", -s)]
        pair.append(net.send(came, came, "core"))
    finish(swaps)
    pair[0].wait()
    left = unit(dotf(inv[0], dotf(cross[...], dotf(inv[1], init[...], 0, 0), 1, 0), 1, 0))
    scale = 1.0 / math.sqrt(inv.shape[1])
    geno_weights = dotf(inv[0], left, 0, 0)
    right = unit(dotf(inv[1], dotf(cross[...], geno_weights, 0, 0), 1, 0))
    trait_weights = dotf(inv[1], right, 0, 0)
    finish(pair[1:])
    flat = full[...].reshape(640, 1024)
    tscore = dotf(flat[:, 512:1024], trait_weights * scale, 1, 0).astype(jnp.bfloat16)
    trait_t = tscore.T

    def put(target, at, lhs, rhs):
        width = rhs.shape[1]
        target[:, :, :, at : at + width] = jnp.dot(lhs, rhs, preferred_element_type=F32).reshape(
            4, 8, 8, width
        )

    scores[:, 256:512] = tscore
    running = {}
    geno_t = None
    for turn in TURNS:
        if turn not in running:
            make, _, first, count, genos = STREAMS[turn]
            target = parts[turn][0]
            for at in range(0, count, 256):
                put(target, at, trait_t, traits[:, first + at : first + at + 256])
            if genos:
                gscore = dotf(flat[:, 0:512], geno_weights * scale, 1, 0).astype(jnp.bfloat16)
                scores[:, 0:256] = gscore
                geno_t = gscore.T
            for at in range(0, genos, 256):
                put(target, count + at, geno_t, std[:, at : at + 256])
            running[turn] = make(net, *parts[turn])
        next(running[turn], None)
    together(running.values())
    scale = 1.0 / math.sqrt(people)
    for (_, _, first, count, genos), part_of in zip(STREAMS, parts):
        loads[:, 512 + first : 512 + first + count] = part_of[4][:, 0:count] * scale
        if genos:
            loads[:, 0:512] = part_of[4][:, count : count + genos] * scale


def cca(people, geno, freq, traits, gsk, tsk, init):
    vm, far = pl.BlockSpec(memory_space=pltpu.VMEM), pl.BlockSpec(memory_space=pl.ANY)
    sems = 4 + 12 + 1 + 2 * (2 * (3 + 3 + 7)) + 3 + 1 + 4 + 3 + (6 + 14) + (6 + 7) + 2 * (14 + 3)
    return pl.pallas_call(
        functools.partial(cca_kernel, people),
        out_shape=[
            jax.ShapeDtypeStruct((640, 512), jnp.bfloat16),
            jax.ShapeDtypeStruct((8, 4608), F32),
        ],
        in_specs=[far, vm, far, far, far, vm],
        out_specs=[vm] * 2,
        scratch_shapes=[
            pltpu.VMEM((640, 512), jnp.int32),
            pltpu.VMEM((640, 4096), jnp.bfloat16),
            pltpu.VMEM((512, 512), jnp.bfloat16),
            pltpu.VMEM((4096, 512), jnp.bfloat16),
            pltpu.VMEM((640, 512), jnp.bfloat16),
            pltpu.VMEM((4, 320, 256), F32),
            pltpu.VMEM((4, 320, 256), F32),
            pltpu.VMEM((4, 320, 256), F32),
            pltpu.VMEM((3, 4, 80, 256), F32),
            pltpu.VMEM((2, 80, 1024), F32),
            pltpu.VMEM((2304, 128), F32),
            *GRAM_SCRATCH,
            *GRAM_SCRATCH,
            pltpu.VMEM((512, 1024), F32),
            pltpu.VMEM((128, 256), F32),
            pltpu.VMEM((2, 512, 512), F32),
            pltpu.VMEM((512, 512), F32),
            pltpu.VMEM((8, 80, 1024), F32),
            *[buffer for _, scratch, _, count, genos in STREAMS for buffer in scratch(count + genos)],
            pltpu.SemaphoreType.DMA((sems,)),
            pltpu.SemaphoreType.DMA((sems,)),
            pltpu.SemaphoreType.DMA((6,)),
        ],
        compiler_params=pltpu.CompilerParams(
            collective_id=1, has_side_effects=True, vmem_limit_bytes=60 << 20
        ),
        name="cca",
    )(geno, freq, traits, gsk, tsk, init)


def on_device(genotypes, frequencies, traits, geno_sketch, trait_sketch, initial):
    people = genotypes.shape[0] * lax.axis_size("rows")
    scores, loads = cca(
        people, genotypes, frequencies[None, :], traits, geno_sketch, trait_sketch, initial
    )
    pairs, width = initial.shape[1], genotypes.shape[1]
    return (scores[:, :pairs], scores[:, pairs:], loads[:, :width], loads[:, width:])


def solution(mesh):
    placed = (
        P("rows", "cols"),
        P("cols"),
        P("rows", "cols"),
        P("cols", None),
        P("cols", None),
        P(),
    )
    return jax.shard_map(
        on_device,
        mesh=mesh,
        in_specs=placed,
        out_specs=(P("rows", None), P("rows", None), P("rows", "cols"), P("rows", "cols")),
        check_vma=False,
    )
```

```python
import functools
import math

import jax
import jax.numpy as jnp
from jax import lax
from jax.experimental import pallas as pl
from jax.experimental.pallas import tpu as pltpu
from jax.sharding import PartitionSpec as P

HI=lax.Precision.HIGHEST
F32=jnp.float32
def dotf(a,b,ca,cb):
    return lax.dot_general(a,b,(((ca,),(cb,)),((),())),precision=HI,preferred_element_type=F32)


def factor(d_ref):
    row = lax.broadcasted_iota(jnp.int32, (8, 128), 0)
    lane = lax.broadcasted_iota(jnp.int32, (8, 128), 1)
    for p in range(16):
        lo, hi = 8 * p, 8 * p + 8
        work = d_ref[lo:hi, 0:128]
        cell = {}
        for j in range(8):
            column = jnp.broadcast_to(work[:, lo + j : lo + j + 1], (8, 128))
            for i in range(8):
                cell[i, j] = column[i : i + 1, :]
        pivot = (lane >= lo) & (lane < hi)
        work = jnp.where(pivot, jnp.where(lane - lo == row, 1.0, 0.0), work)
        final = work
        for j in range(8):
            inv, root = 1.0 / cell[j, j], lax.rsqrt(cell[j, j])
            here = work[j : j + 1, :]
            final = jnp.where(row == j, jnp.broadcast_to(here * root, (8, 128)), final)
            others = [i for i in range(8) if i != j]
            ratio = {i: cell[i, j] * inv for i in others}
            for b in range(j + 1, 8):
                top = cell[j, b]
                for i in others:
                    cell[i, b] = cell[i, b] - ratio[i] * top
                cell[j, b] = top * inv
            factors = jnp.zeros((8, 128), F32)
            for i in others:
                factors = jnp.where(row == i, jnp.broadcast_to(ratio[i], (8, 128)), factors)
            here = jnp.broadcast_to(here, (8, 128))
            work = jnp.where(row == j, here * inv, work - factors * here)
        d_ref[lo:hi, 128:256] = jnp.where(lane < hi, final, 0.0)
        for g in range(p + 1, 16):
            group = slice(8 * g, 8 * g + 8)
            old = d_ref[group, 0:128]
            new = jnp.where(pivot, 0.0, old)
            for j in range(8):
                new = new - old[:, lo + j : lo + j + 1] * work[j : j + 1, :]
            d_ref[group, 0:128] = new


MESH = pl.DeviceIdType.MESH


class Place:
    def __init__(self):
        rows, cols = lax.axis_index("rows"), lax.axis_index("cols")
        self.x, self.core = lax.div(cols, 2), lax.rem(cols, 2)
        self.y, self.z = lax.div(rows, 8), lax.rem(rows, 8)

    def ring(self, axis):
        return (self.z, 8) if axis == "z" else (getattr(self, axis), 4)

    def other(self, axis, step):
        here, size = self.ring(axis)
        return lax.rem(here + step + size, size)

    def device(self, axis, step):
        at = {"x": self.x, "y": self.y, "z": self.z, "core": self.core}
        at[axis] = 1 - self.core if axis == "core" else self.other(axis, step)
        return (at["y"] * 8 + at["z"], at["x"] * 2 + at["core"])


class Net:
    def __init__(self, place, sends, recvs):
        self.place, self.sends, self.recvs, self.count = place, sends, recvs, 0

    def greet(self, axes):
        barrier = pltpu.get_barrier_semaphore()
        partners = [(a, s) for a in axes for s in range(1, {"core": 2, "z": 8}.get(a, 4))]
        for axis, step in partners:
            pl.semaphore_signal(
                barrier, inc=1, device_id=self.place.device(axis, step), device_id_type=MESH
            )
        pl.semaphore_wait(barrier, len(partners))

    def send(self, source, target, axis, step=1):
        copy = self.plan(source, target, axis, step)
        copy.start()
        return copy

    def plan(self, source, target, axis, step=1):
        slot = self.count
        self.count += 1
        return pltpu.make_async_remote_copy(
            src_ref=source,
            dst_ref=target,
            send_sem=self.sends.at[slot],
            recv_sem=self.recvs.at[slot],
            device_id=self.place.device(axis, step),
            device_id_type=MESH,
        )

    def scatter(self, axis, part, landing):
        size = self.place.ring(axis)[1]
        order = sorted(range(1, size), key=lambda s: -min(s, size - s))
        return [
            self.send(part(self.place.other(axis, s)), landing.at[s - 1], axis, s) for s in order
        ]

    def gather(self, axis, own):
        size = self.place.ring(axis)[1]
        order = sorted(range(1, size), key=lambda s: -min(s, size - s))
        return [self.send(own, own, axis, s) for s in order]


def ring_scatter(net, axis, part, lands):
    place = net.place
    size = place.ring(axis)[1]
    turns = size // 2
    ways = ((0, 1), (1, size - 1))
    flight = {d: {d: net.send(part(place.other(axis, turns), d), lands(d, 0, d), axis, s)} for d, s in ways}
    sent = [flight[d][d] for d, _ in ways]
    for hop in range(1, turns):
        leaving = {0: {}, 1: {}}
        if hop == 1:
            for d, s in ways:
                chunk = place.other(axis, turns - 1 if d == 0 else 1 - turns)
                leaving[d][1 - d] = net.send(part(chunk, 1 - d), lands(d, 1, 1 - d), axis, s)
        yield
        for first in (True, False):
            for d, s in ways:
                h = d if first else 1 - d
                if h not in flight[d]:
                    continue
                chunk = place.other(axis, turns - hop if d == 0 else hop - turns)
                flight[d][h].wait_recv()
                passed, mine = lands(d, hop - 1, h), part(chunk, h)
                passed[...] = passed[...] + mine[...]
                leaving[d][h] = net.send(passed, lands(d, hop, h), axis, s)
        flight = leaving
        sent += [flight[d][h] for d in (0, 1) for h in (0, 1)]
    yield
    for d, _ in ways:
        for h in (0, 1):
            flight[d][h].wait_recv()
    for copy in sent:
        copy.wait_send()


def finish(copies):
    for copy in copies:
        copy.wait()


def rows_of(index, count):
    return pl.ds(pl.multiple_of(index * count, count), count)


def total_of(landing):
    total = landing[0]
    for s in range(1, landing.shape[0]):
        total = total + landing[s]
    return total


def gram_stream(net, axes, source, land1, part1, land2, part2, land3, out3, out2, out1):
    place = net.place
    (i1, s1), (i2, s2), (i3, s3) = (place.ring(axis) for axis in axes)
    r1, r2, r3 = part1.shape[0], land2.shape[1], land3.shape[1]
    copies = net.scatter(axes[0], lambda i: source.at[rows_of(i, r1)], land1)
    yield
    finish(copies)
    part1[...] = source[rows_of(i1, r1)] + total_of(land1)
    copies = net.scatter(axes[1], lambda i: part1.at[rows_of(i, r2)], land2)
    if r3 * s3 > r2:
        part2[r2 : r3 * s3] = jnp.zeros((r3 * s3 - r2, 128), F32)
    yield
    finish(copies)
    part2[0:r2] = part1[rows_of(i2, r2)] + total_of(land2)
    copies = net.scatter(axes[2], lambda i: part2.at[rows_of(i, r3)], land3)
    yield
    finish(copies)
    out3[rows_of(i3, r3)] = part2[rows_of(i3, r3)] + total_of(land3)
    copies = net.gather(axes[2], out3.at[rows_of(i3, r3)])
    yield
    finish(copies)
    out2[i2] = out3[0:r2]
    copies = net.gather(axes[1], out2.at[i2])
    yield
    finish(copies)
    out1[i1] = out2[...]
    copies = net.gather(axes[0], out1.at[i1])
    yield
    finish(copies)


GRAMS = (("xyz", 0, 1024), ("yxz", 1024, 1024), ("zxy", 2048, 256))


def gram_scratch(axes, rows):
    s1, s2, s3 = (8 if axis == "z" else 4 for axis in axes)
    r1, r2 = rows // s1, rows // s1 // s2
    r3 = -(-r2 // (8 * s3)) * 8
    shapes = (
        (s1 - 1, r1),
        (r1,),
        (s2 - 1, r2),
        (r3 * s3,),
        (s3 - 1, r3),
        (r3 * s3,),
        (s2, r2),
        (s1, s2, r2),
    )
    return [pltpu.VMEM((*shape, 128), F32) for shape in shapes]


UPPER = [(i, j) for j in range(4) for i in range(j + 1)]


def together(streams):
    streams = list(streams)
    while streams:
        alive = []
        for stream in streams:
            try:
                next(stream)
                alive.append(stream)
            except StopIteration:
                pass
        streams = alive


def unit(v):
    return v * lax.rsqrt(jnp.mean(v * v, axis=0, keepdims=True) + 1e-06)


def rows_first(net, source, land1, part1, land2, out):
    place, half = net.place, source.shape[-1] // 2
    yield from ring_scatter(
        net,
        "y",
        lambda i, h: source.at[i, :, :, half * h : half * h + half],
        lambda d, hop, h: land1.at[d, hop, :, :, half * h : half * h + half],
    )
    part1[...] = source[place.y] + land1[0, 1] + land1[1, 1]
    copies = net.scatter("z", lambda i: part1.at[i], land2)
    yield
    finish(copies)
    out[...] = part1[place.z] + total_of(land2)


def rings_only(net, source, land1, part1, land2, out):
    place, half = net.place, source.shape[-1] // 2
    yield from ring_scatter(
        net,
        "y",
        lambda i, h: source.at[i, :, :, half * h : half * h + half],
        lambda d, hop, h: land1.at[d, hop, :, :, half * h : half * h + half],
    )
    part1[...] = source[place.y] + land1[0, 1] + land1[1, 1]
    yield from ring_scatter(
        net,
        "z",
        lambda i, h: part1.at[i, :, half * h : half * h + half],
        lambda d, hop, h: land2.at[d, hop, :, half * h : half * h + half],
    )
    out[...] = part1[place.z] + land2[0, 3] + land2[1, 3]


def ring_first(net, source, land1, part1, land2, out):
    place, half = net.place, source.shape[-1] // 2
    yield from ring_scatter(
        net,
        "z",
        lambda i, h: source.at[:, i, :, half * h : half * h + half],
        lambda d, hop, h: land1.at[d, hop, :, :, half * h : half * h + half],
    )
    part1[...] = source[:, place.z] + land1[0, 3] + land1[1, 3]
    copies = net.scatter("y", lambda i: part1.at[i], land2)
    yield
    finish(copies)
    out[...] = part1[place.y] + total_of(land2)


def rows_scratch(width):
    return [
        pltpu.VMEM((4, 8, 8, width), F32),
        pltpu.VMEM((2, 2, 8, 8, width), F32),
        pltpu.VMEM((8, 8, width), F32),
        pltpu.VMEM((7, 8, width), F32),
        pltpu.VMEM((8, width), F32),
    ]


def rings_scratch(width):
    return [
        pltpu.VMEM((4, 8, 8, width), F32),
        pltpu.VMEM((2, 2, 8, 8, width), F32),
        pltpu.VMEM((8, 8, width), F32),
        pltpu.VMEM((2, 4, 8, width), F32),
        pltpu.VMEM((8, width), F32),
    ]


def ring_scratch(width):
    return [
        pltpu.VMEM((4, 8, 8, width), F32),
        pltpu.VMEM((2, 4, 4, 8, width), F32),
        pltpu.VMEM((4, 8, width), F32),
        pltpu.VMEM((3, 8, width), F32),
        pltpu.VMEM((8, width), F32),
    ]


STREAMS = (
    (rings_only, rings_scratch, 0, 1536, 0),
    (ring_first, ring_scratch, 1536, 1024, 0),
    (ring_first, ring_scratch, 2560, 512, 512),
    (rows_first, rows_scratch, 3072, 1024, 0),
)
TURNS = (0, 1, 2, 1, 0, 3, 2, 1, 2, 0, 3, 1, 2, 0, 3)


def invert(a_ref, d_ref, done):
    eye = (
        lax.broadcasted_iota(jnp.int32, (128, 128), 0) == lax.broadcasted_iota(jnp.int32, (128, 128), 1)
    ).astype(F32)
    a_ref[:, 512:1024] = jnp.zeros((512, 512), F32)
    for k in range(4):
        a_ref[128 * k : 128 * k + 128, 512 + 128 * k : 640 + 128 * k] = eye

    def body(k, _):
        for kk in range(4):

            @pl.when(k == kk)
            def _():
                d_ref[:, 0:128] = a_ref[128 * kk : 128 * kk + 128, 128 * kk : 128 * kk + 128]

        factor(d_ref)
        for kk in range(4):

            @pl.when(k == kk)
            def _():
                lo = 128 * (kk + 1)
                block = slice(128 * kk, 128 * kk + 128)
                panel = dotf(d_ref[:, 128:256], a_ref[block, lo : lo + 512], 1, 0)
                a_ref[block, lo : lo + 512] = panel
                done(kk)
                if kk < 3:
                    a_ref[lo:512, lo : lo + 512] = a_ref[lo:512, lo : lo + 512] - dotf(
                        panel[:, : 512 - lo].T, panel, 1, 0
                    )

        return 0

    lax.fori_loop(0, 4, body, 0)


def cca_kernel(people, geno_in, freq, traits_in, gsk_in, tsk_in, init, scores, loads, *scratch):
    geno, traits, gsk, tsk, std, give, take, held, lands, both, source = scratch[:11]
    grams = [scratch[11 + 8 * s : 19 + 8 * s] for s in range(3)]
    a_ref, d_ref, inv, cross, full = scratch[35:40]
    parts = [scratch[40 + 5 * s : 45 + 5 * s] for s in range(4)]
    sends, recvs, loaded = scratch[60:63]
    place = Place()
    net = Net(place, sends, recvs)
    x, k = place.x, place.core
    cols = pl.ds(pl.multiple_of(256 * k, 256), 256)

    def load(slot, origin, target):
        copy = pltpu.make_async_copy(origin, target, loaded.at[slot])
        copy.start()
        return copy

    def half_load(slot, half):
        rows = rows_of(half, 320)
        return load(slot, traits_in.at[rows], traits.at[rows])

    loads_of = [
        load(0, tsk_in.at[:, 0:256], tsk.at[:, 0:256]),
        half_load(1, 1 - k),
        load(2, geno_in, geno),
        load(3, tsk_in.at[:, 256:512], tsk.at[:, 256:512]),
        load(4, gsk_in, gsk),
        half_load(5, k),
    ]
    net.greet(("core", "x", "y", "z"))

    def piece(half, j):
        rows = rows_of(half, 320)
        if j < 2:
            return jnp.dot(traits[rows], tsk[:, 256 * j : 256 * j + 256], preferred_element_type=F32)
        j -= 2
        return jnp.dot(std[rows], gsk[:, 256 * j : 256 * j + 256], preferred_element_type=F32)

    copies = []
    finish(loads_of[:2])
    for j in range(4):
        if j == 1:
            loads_of[3].wait()
        if j == 2:
            finish([loads_of[2], loads_of[4]])
            spread = lax.rsqrt(2.0 * freq[...] * (1.0 - freq[...]))
            std[...] = ((geno[...].astype(F32) - 2.0 * freq[...]) * spread).astype(jnp.bfloat16)
        give[j] = piece(1 - k, j)
        copies.append(net.send(give.at[j], take.at[j], "core"))
    loads_of[5].wait()

    def part(j, step):
        return held.at[j, rows_of(place.other("x", step), 80)]

    far, near = [], []
    for j in range(4):
        mine = piece(k, j)
        copies[j].wait()
        held[j] = mine + take[j]
        toward, away = (1, 3) if j < 2 else (3, 1)
        far.append(net.send(part(j, 2), lands.at[0, j], "x", toward))
        near.append(net.send(part(j, away), lands.at[1, j], "x", away))
    passing = []
    for j in range(4):
        toward = 1 if j < 2 else 3
        far[j].wait_recv()
        lands[0, j] = lands[0, j] + part(j, toward)[...]
        passing.append(net.send(lands.at[0, j], lands.at[2, j], "x", toward))
    for j in range(4):
        near[j].wait_recv()
        passing[j].wait_recv()
        at = 512 + 256 * j if j < 2 else 256 * j - 512
        both[k, :, at : at + 256] = part(j, 0)[...] + lands[1, j] + lands[2, j]
    copy = net.send(both.at[k], both.at[k], "core")
    for other in far + near + passing:
        other.wait_send()
    copy.wait()
    flat = both[...].reshape(160, 1024)
    view = both[:, :, pl.ds(pl.multiple_of(512 * k, 512), 512)].reshape(160, 512)
    side = both[:, :, pl.ds(pl.multiple_of(512 + 256 * k, 256), 256)].reshape(160, 256)
    gram = dotf(view.T, view, 1, 0)
    for t, (i, j) in enumerate(UPPER):
        source[128 * t : 128 * t + 128] = gram[128 * i : 128 * i + 128, 128 * j : 128 * j + 128]
    crossed = dotf(flat[:, 0:512].T, side, 1, 0)
    for j in range(2):
        for i in range(4):
            t = 10 + 4 * j + i
            source[128 * t : 128 * t + 128] = crossed[128 * i : 128 * i + 128, 128 * j : 128 * j + 128]
    together(
        [
            gram_stream(net, axes, source.at[first : first + rows], *buffers)
            for (axes, first, rows), buffers in zip(GRAMS, grams)
        ]
    )
    for (_, first, rows), buffers in zip(GRAMS, grams):
        s1, s2, r2 = buffers[7].shape[:3]
        for i in range(s1):
            for j in range(s2):
                at = first + r2 * (s2 * i + j)
                source[at : at + r2] = buffers[7][i, j]

    full[k * 4 + x] = both[k]
    full[(1 - k) * 4 + x] = both[1 - k]
    here = full.at[k * 4 + x]
    across = [net.send(here, here, "x", s) for s in (2, 1, 3)]
    scale = 1.0 / people
    a_ref[:, 0:512] = jnp.zeros((512, 512), F32)
    for t, (i, j) in enumerate(UPPER):
        a_ref[128 * i : 128 * i + 128, 128 * j : 128 * j + 128] = source[128 * t : 128 * t + 128] * scale
    for j in range(2):
        at = pl.ds(pl.multiple_of(256 * k + 128 * j, 128), 128)
        for i in range(4):
            t = 10 + 4 * j + i
            cross[128 * i : 128 * i + 128, at] = source[128 * t : 128 * t + 128] * scale
    pair = [net.send(cross.at[:, cols], cross.at[:, cols], "core")]
    swaps = []
    for i in range(4):
        block = (slice(128 * i, 128 * i + 128), slice(0, 128 * i + 128))
        swaps.append(net.plan(inv.at[(k, *block)], inv.at[(k, *block)], "core"))
        if i < 3:
            rest = slice(128 * i + 128, 512)
            for v in range(2):
                inv[v, 128 * i : 128 * i + 128, rest] = jnp.zeros((128, 384 - 128 * i), F32)

    def done(i):
        block = (slice(128 * i, 128 * i + 128), slice(0, 128 * i + 128))
        inv[(k, *block)] = a_ref[128 * i : 128 * i + 128, 512 : 640 + 128 * i]
        swaps[i].start()

    invert(a_ref, d_ref, done)
    for s, copy in zip((2, 1, 3), across):
        copy.wait()
        came = full.at[k * 4 + place.other("x", -s)]
        pair.append(net.send(came, came, "core"))
    finish(swaps)
    pair[0].wait()
    left = unit(dotf(inv[0], dotf(cross[...], dotf(inv[1], init[...], 0, 0), 1, 0), 1, 0))
    scale = 1.0 / math.sqrt(inv.shape[1])
    geno_weights = dotf(inv[0], left, 0, 0)
    right = unit(dotf(inv[1], dotf(cross[...], geno_weights, 0, 0), 1, 0))
    trait_weights = dotf(inv[1], right, 0, 0)
    finish(pair[1:])
    flat = full[...].reshape(640, 1024)
    tscore = dotf(flat[:, 512:1024], trait_weights * scale, 1, 0).astype(jnp.bfloat16)
    trait_t = tscore.T

    def put(target, at, lhs, rhs):
        width = rhs.shape[1]
        target[:, :, :, at : at + width] = jnp.dot(lhs, rhs, preferred_element_type=F32).reshape(
            4, 8, 8, width
        )

    scores[:, 256:512] = tscore
    running = {}
    geno_t = None
    for turn in TURNS:
        if turn not in running:
            make, _, first, count, genos = STREAMS[turn]
            target = parts[turn][0]
            for at in range(0, count, 256):
                put(target, at, trait_t, traits[:, first + at : first + at + 256])
            if genos:
                gscore = dotf(flat[:, 0:512], geno_weights * scale, 1, 0).astype(jnp.bfloat16)
                scores[:, 0:256] = gscore
                geno_t = gscore.T
            for at in range(0, genos, 256):
                put(target, count + at, geno_t, std[:, at : at + 256])
            running[turn] = make(net, *parts[turn])
        next(running[turn], None)
    together(running.values())
    scale = 1.0 / math.sqrt(people)
    for (_, _, first, count, genos), part_of in zip(STREAMS, parts):
        loads[:, 512 + first : 512 + first + count] = part_of[4][:, 0:count] * scale
        if genos:
            loads[:, 0:512] = part_of[4][:, count : count + genos] * scale


def cca(people, geno, freq, traits, gsk, tsk, init):
    vm, far = pl.BlockSpec(memory_space=pltpu.VMEM), pl.BlockSpec(memory_space=pl.ANY)
    sems = 4 + 12 + 1 + 3 * (2 * (3 + 3 + 7)) + 3 + 1 + 4 + 3 + (6 + 14) + (6 + 7) + 2 * (14 + 3)
    return pl.pallas_call(
        functools.partial(cca_kernel, people),
        out_shape=[
            jax.ShapeDtypeStruct((640, 512), jnp.bfloat16),
            jax.ShapeDtypeStruct((8, 4608), F32),
        ],
        in_specs=[far, vm, far, far, far, vm],
        out_specs=[vm] * 2,
        scratch_shapes=[
            pltpu.VMEM((640, 512), jnp.int32),
            pltpu.VMEM((640, 4096), jnp.bfloat16),
            pltpu.VMEM((512, 512), jnp.bfloat16),
            pltpu.VMEM((4096, 512), jnp.bfloat16),
            pltpu.VMEM((640, 512), jnp.bfloat16),
            pltpu.VMEM((4, 320, 256), F32),
            pltpu.VMEM((4, 320, 256), F32),
            pltpu.VMEM((4, 320, 256), F32),
            pltpu.VMEM((3, 4, 80, 256), F32),
            pltpu.VMEM((2, 80, 1024), F32),
            pltpu.VMEM((2304, 128), F32),
            *[buffer for axes, _, rows in GRAMS for buffer in gram_scratch(axes, rows)],
            pltpu.VMEM((512, 1024), F32),
            pltpu.VMEM((128, 256), F32),
            pltpu.VMEM((2, 512, 512), F32),
            pltpu.VMEM((512, 512), F32),
            pltpu.VMEM((8, 80, 1024), F32),
            *[buffer for _, scratch, _, count, genos in STREAMS for buffer in scratch(count + genos)],
            pltpu.SemaphoreType.DMA((sems,)),
            pltpu.SemaphoreType.DMA((sems,)),
            pltpu.SemaphoreType.DMA((6,)),
        ],
        compiler_params=pltpu.CompilerParams(
            collective_id=1, has_side_effects=True, vmem_limit_bytes=60 << 20
        ),
        name="cca",
    )(geno, freq, traits, gsk, tsk, init)


def on_device(genotypes, frequencies, traits, geno_sketch, trait_sketch, initial):
    people = genotypes.shape[0] * lax.axis_size("rows")
    scores, loads = cca(
        people, genotypes, frequencies[None, :], traits, geno_sketch, trait_sketch, initial
    )
    pairs, width = initial.shape[1], genotypes.shape[1]
    return (scores[:, :pairs], scores[:, pairs:], loads[:, :width], loads[:, width:])


def solution(mesh):
    placed = (
        P("rows", "cols"),
        P("cols"),
        P("rows", "cols"),
        P("cols", None),
        P("cols", None),
        P(),
    )
    return jax.shard_map(
        on_device,
        mesh=mesh,
        in_specs=placed,
        out_specs=(P("rows", None), P("rows", None), P("rows", "cols"), P("rows", "cols")),
        check_vma=False,
    )
```

```python
import functools
import math

import jax
import jax.numpy as jnp
from jax import lax
from jax.experimental import pallas as pl
from jax.experimental.pallas import tpu as pltpu
from jax.sharding import PartitionSpec as P

HI=lax.Precision.HIGHEST
F32=jnp.float32
def dotf(a,b,ca,cb):
    return lax.dot_general(a,b,(((ca,),(cb,)),((),())),precision=HI,preferred_element_type=F32)


def factor(d_ref):
    row = lax.broadcasted_iota(jnp.int32, (8, 128), 0)
    lane = lax.broadcasted_iota(jnp.int32, (8, 128), 1)
    for p in range(16):
        lo, hi = 8 * p, 8 * p + 8
        work = d_ref[lo:hi, 0:128]
        cell = {}
        for j in range(8):
            column = jnp.broadcast_to(work[:, lo + j : lo + j + 1], (8, 128))
            for i in range(8):
                cell[i, j] = column[i : i + 1, :]
        pivot = (lane >= lo) & (lane < hi)
        work = jnp.where(pivot, jnp.where(lane - lo == row, 1.0, 0.0), work)
        final = work
        for j in range(8):
            inv, root = 1.0 / cell[j, j], lax.rsqrt(cell[j, j])
            here = work[j : j + 1, :]
            final = jnp.where(row == j, jnp.broadcast_to(here * root, (8, 128)), final)
            others = [i for i in range(8) if i != j]
            ratio = {i: cell[i, j] * inv for i in others}
            for b in range(j + 1, 8):
                top = cell[j, b]
                for i in others:
                    cell[i, b] = cell[i, b] - ratio[i] * top
                cell[j, b] = top * inv
            factors = jnp.zeros((8, 128), F32)
            for i in others:
                factors = jnp.where(row == i, jnp.broadcast_to(ratio[i], (8, 128)), factors)
            here = jnp.broadcast_to(here, (8, 128))
            work = jnp.where(row == j, here * inv, work - factors * here)
        d_ref[lo:hi, 128:256] = jnp.where(lane < hi, final, 0.0)
        for g in range(p + 1, 16):
            group = slice(8 * g, 8 * g + 8)
            old = d_ref[group, 0:128]
            new = jnp.where(pivot, 0.0, old)
            for j in range(8):
                new = new - old[:, lo + j : lo + j + 1] * work[j : j + 1, :]
            d_ref[group, 0:128] = new


MESH = pl.DeviceIdType.MESH


class Place:
    def __init__(self):
        rows, cols = lax.axis_index("rows"), lax.axis_index("cols")
        self.x, self.core = lax.div(cols, 2), lax.rem(cols, 2)
        self.y, self.z = lax.div(rows, 8), lax.rem(rows, 8)

    def ring(self, axis):
        return (self.z, 8) if axis == "z" else (getattr(self, axis), 4)

    def other(self, axis, step):
        here, size = self.ring(axis)
        return lax.rem(here + step + size, size)

    def device(self, axis, step):
        at = {"x": self.x, "y": self.y, "z": self.z, "core": self.core}
        at[axis] = 1 - self.core if axis == "core" else self.other(axis, step)
        return (at["y"] * 8 + at["z"], at["x"] * 2 + at["core"])


class Net:
    def __init__(self, place, sends, recvs):
        self.place, self.sends, self.recvs, self.count = place, sends, recvs, 0

    def greet(self, axes):
        barrier = pltpu.get_barrier_semaphore()
        partners = [(a, s) for a in axes for s in range(1, {"core": 2, "z": 8}.get(a, 4))]
        for axis, step in partners:
            pl.semaphore_signal(
                barrier, inc=1, device_id=self.place.device(axis, step), device_id_type=MESH
            )
        pl.semaphore_wait(barrier, len(partners))

    def send(self, source, target, axis, step=1):
        copy = self.plan(source, target, axis, step)
        copy.start()
        return copy

    def plan(self, source, target, axis, step=1):
        slot = self.count
        self.count += 1
        return pltpu.make_async_remote_copy(
            src_ref=source,
            dst_ref=target,
            send_sem=self.sends.at[slot],
            recv_sem=self.recvs.at[slot],
            device_id=self.place.device(axis, step),
            device_id_type=MESH,
        )

    def scatter(self, axis, part, landing):
        size = self.place.ring(axis)[1]
        order = sorted(range(1, size), key=lambda s: -min(s, size - s))
        return [
            self.send(part(self.place.other(axis, s)), landing.at[s - 1], axis, s) for s in order
        ]

    def gather(self, axis, own):
        size = self.place.ring(axis)[1]
        order = sorted(range(1, size), key=lambda s: -min(s, size - s))
        return [self.send(own, own, axis, s) for s in order]


def ring_scatter(net, axis, part, lands):
    place = net.place
    size = place.ring(axis)[1]
    turns = size // 2
    ways = ((0, 1), (1, size - 1))
    flight = {d: {d: net.send(part(place.other(axis, turns), d), lands(d, 0, d), axis, s)} for d, s in ways}
    sent = [flight[d][d] for d, _ in ways]
    for hop in range(1, turns):
        leaving = {0: {}, 1: {}}
        if hop == 1:
            for d, s in ways:
                chunk = place.other(axis, turns - 1 if d == 0 else 1 - turns)
                leaving[d][1 - d] = net.send(part(chunk, 1 - d), lands(d, 1, 1 - d), axis, s)
        yield
        for first in (True, False):
            for d, s in ways:
                h = d if first else 1 - d
                if h not in flight[d]:
                    continue
                chunk = place.other(axis, turns - hop if d == 0 else hop - turns)
                flight[d][h].wait_recv()
                passed, mine = lands(d, hop - 1, h), part(chunk, h)
                passed[...] = passed[...] + mine[...]
                leaving[d][h] = net.send(passed, lands(d, hop, h), axis, s)
        flight = leaving
        sent += [flight[d][h] for d in (0, 1) for h in (0, 1)]
    yield
    for d, _ in ways:
        for h in (0, 1):
            flight[d][h].wait_recv()
    for copy in sent:
        copy.wait_send()


def finish(copies):
    for copy in copies:
        copy.wait()


def rows_of(index, count):
    return pl.ds(pl.multiple_of(index * count, count), count)


def total_of(landing):
    total = landing[0]
    for s in range(1, landing.shape[0]):
        total = total + landing[s]
    return total


def gram_stream(net, axes, source, land1, part1, land2, part2, land3, out3, out2, out1):
    place = net.place
    (i1, s1), (i2, s2), (i3, s3) = (place.ring(axis) for axis in axes)
    r1, r2, r3 = part1.shape[0], land2.shape[1], land3.shape[1]
    copies = net.scatter(axes[0], lambda i: source.at[rows_of(i, r1)], land1)
    yield
    finish(copies)
    part1[...] = source[rows_of(i1, r1)] + total_of(land1)
    copies = net.scatter(axes[1], lambda i: part1.at[rows_of(i, r2)], land2)
    if r3 * s3 > r2:
        part2[r2 : r3 * s3] = jnp.zeros((r3 * s3 - r2, 128), F32)
    yield
    finish(copies)
    part2[0:r2] = part1[rows_of(i2, r2)] + total_of(land2)
    copies = net.scatter(axes[2], lambda i: part2.at[rows_of(i, r3)], land3)
    yield
    finish(copies)
    out3[rows_of(i3, r3)] = part2[rows_of(i3, r3)] + total_of(land3)
    copies = net.gather(axes[2], out3.at[rows_of(i3, r3)])
    yield
    finish(copies)
    out2[i2] = out3[0:r2]
    copies = net.gather(axes[1], out2.at[i2])
    yield
    finish(copies)
    out1[i1] = out2[...]
    copies = net.gather(axes[0], out1.at[i1])
    yield
    finish(copies)


GRAMS = (("xyz", 0, 1024), ("yxz", 1024, 1024), ("zxy", 2048, 256))


def gram_scratch(axes, rows):
    s1, s2, s3 = (8 if axis == "z" else 4 for axis in axes)
    r1, r2 = rows // s1, rows // s1 // s2
    r3 = -(-r2 // (8 * s3)) * 8
    shapes = (
        (s1 - 1, r1),
        (r1,),
        (s2 - 1, r2),
        (r3 * s3,),
        (s3 - 1, r3),
        (r3 * s3,),
        (s2, r2),
        (s1, s2, r2),
    )
    return [pltpu.VMEM((*shape, 128), F32) for shape in shapes]


UPPER = [(i, j) for j in range(4) for i in range(j + 1)]


def together(streams):
    streams = list(streams)
    while streams:
        alive = []
        for stream in streams:
            try:
                next(stream)
                alive.append(stream)
            except StopIteration:
                pass
        streams = alive


def unit(v):
    return v * lax.rsqrt(jnp.mean(v * v, axis=1, keepdims=True) + 1e-06)


def rows_first(net, source, land1, part1, land2, out):
    place, half = net.place, source.shape[-1] // 2
    yield from ring_scatter(
        net,
        "y",
        lambda i, h: source.at[i, :, :, half * h : half * h + half],
        lambda d, hop, h: land1.at[d, hop, :, :, half * h : half * h + half],
    )
    part1[...] = source[place.y] + land1[0, 1] + land1[1, 1]
    copies = net.scatter("z", lambda i: part1.at[i], land2)
    yield
    finish(copies)
    out[...] = part1[place.z] + total_of(land2)


def rings_only(net, source, land1, part1, land2, out):
    place, half = net.place, source.shape[-1] // 2
    yield from ring_scatter(
        net,
        "y",
        lambda i, h: source.at[i, :, :, half * h : half * h + half],
        lambda d, hop, h: land1.at[d, hop, :, :, half * h : half * h + half],
    )
    part1[...] = source[place.y] + land1[0, 1] + land1[1, 1]
    yield from ring_scatter(
        net,
        "z",
        lambda i, h: part1.at[i, :, half * h : half * h + half],
        lambda d, hop, h: land2.at[d, hop, :, half * h : half * h + half],
    )
    out[...] = part1[place.z] + land2[0, 3] + land2[1, 3]


def ring_first(net, source, land1, part1, land2, out):
    place, half = net.place, source.shape[-1] // 2
    yield from ring_scatter(
        net,
        "z",
        lambda i, h: source.at[:, i, :, half * h : half * h + half],
        lambda d, hop, h: land1.at[d, hop, :, :, half * h : half * h + half],
    )
    part1[...] = source[:, place.z] + land1[0, 3] + land1[1, 3]
    copies = net.scatter("y", lambda i: part1.at[i], land2)
    yield
    finish(copies)
    out[...] = part1[place.y] + total_of(land2)


def rows_scratch(width):
    return [
        pltpu.VMEM((4, 8, 8, width), F32),
        pltpu.VMEM((2, 2, 8, 8, width), F32),
        pltpu.VMEM((8, 8, width), F32),
        pltpu.VMEM((7, 8, width), F32),
        pltpu.VMEM((8, width), F32),
    ]


def rings_scratch(width):
    return [
        pltpu.VMEM((4, 8, 8, width), F32),
        pltpu.VMEM((2, 2, 8, 8, width), F32),
        pltpu.VMEM((8, 8, width), F32),
        pltpu.VMEM((2, 4, 8, width), F32),
        pltpu.VMEM((8, width), F32),
    ]


def ring_scratch(width):
    return [
        pltpu.VMEM((4, 8, 8, width), F32),
        pltpu.VMEM((2, 4, 4, 8, width), F32),
        pltpu.VMEM((4, 8, width), F32),
        pltpu.VMEM((3, 8, width), F32),
        pltpu.VMEM((8, width), F32),
    ]


STREAMS = (
    (rings_only, rings_scratch, 0, 1536, 0),
    (ring_first, ring_scratch, 1536, 1024, 0),
    (ring_first, ring_scratch, 2560, 512, 512),
    (rows_first, rows_scratch, 3072, 1024, 0),
)
TURNS = (0, 1, 2, 1, 0, 3, 2, 1, 2, 0, 3, 1, 2, 0, 3)


def invert(a_ref, d_ref, done):
    eye = (
        lax.broadcasted_iota(jnp.int32, (128, 128), 0) == lax.broadcasted_iota(jnp.int32, (128, 128), 1)
    ).astype(F32)
    a_ref[:, 512:1024] = jnp.zeros((512, 512), F32)
    for k in range(4):
        a_ref[128 * k : 128 * k + 128, 512 + 128 * k : 640 + 128 * k] = eye

    def body(k, _):
        for kk in range(4):

            @pl.when(k == kk)
            def _():
                d_ref[:, 0:128] = a_ref[128 * kk : 128 * kk + 128, 128 * kk : 128 * kk + 128]

        factor(d_ref)
        for kk in range(4):

            @pl.when(k == kk)
            def _():
                lo = 128 * (kk + 1)
                block = slice(128 * kk, 128 * kk + 128)
                panel = dotf(d_ref[:, 128:256], a_ref[block, lo : lo + 512], 1, 0)
                a_ref[block, lo : lo + 512] = panel
                done(kk)
                if kk < 3:
                    a_ref[lo:512, lo : lo + 512] = a_ref[lo:512, lo : lo + 512] - dotf(
                        panel[:, : 512 - lo].T, panel, 1, 0
                    )

        return 0

    lax.fori_loop(0, 4, body, 0)


def cca_kernel(people, geno_in, freq, traits_in, gsk_in, tsk_in, init, scores, loads, *scratch):
    geno, traits, gsk, tsk, std, give, take, held, lands, both, source = scratch[:11]
    grams = [scratch[11 + 8 * s : 19 + 8 * s] for s in range(3)]
    a_ref, d_ref, inv, cross, full = scratch[35:40]
    parts = [scratch[40 + 5 * s : 45 + 5 * s] for s in range(4)]
    sends, recvs, loaded = scratch[60:63]
    place = Place()
    net = Net(place, sends, recvs)
    x, k = place.x, place.core
    cols = pl.ds(pl.multiple_of(256 * k, 256), 256)

    def load(slot, origin, target):
        copy = pltpu.make_async_copy(origin, target, loaded.at[slot])
        copy.start()
        return copy

    def half_load(slot, half):
        rows = rows_of(half, 320)
        return load(slot, traits_in.at[rows], traits.at[rows])

    loads_of = [
        load(0, tsk_in.at[:, 0:256], tsk.at[:, 0:256]),
        half_load(1, 1 - k),
        load(2, geno_in, geno),
        load(3, tsk_in.at[:, 256:512], tsk.at[:, 256:512]),
        load(4, gsk_in, gsk),
        half_load(5, k),
    ]
    net.greet(("core", "x", "y", "z"))

    def piece(half, j):
        rows = rows_of(half, 320)
        if j < 2:
            return jnp.dot(traits[rows], tsk[:, 256 * j : 256 * j + 256], preferred_element_type=F32)
        j -= 2
        return jnp.dot(std[rows], gsk[:, 256 * j : 256 * j + 256], preferred_element_type=F32)

    copies = []
    finish(loads_of[:2])
    for j in range(4):
        if j == 1:
            loads_of[3].wait()
        if j == 2:
            finish([loads_of[2], loads_of[4]])
            spread = lax.rsqrt(2.0 * freq[...] * (1.0 - freq[...]))
            std[...] = ((geno[...].astype(F32) - 2.0 * freq[...]) * spread).astype(jnp.bfloat16)
        give[j] = piece(1 - k, j)
        copies.append(net.send(give.at[j], take.at[j], "core"))
    loads_of[5].wait()

    def part(j, step):
        return held.at[j, rows_of(place.other("x", step), 80)]

    far, near = [], []
    for j in range(4):
        mine = piece(k, j)
        copies[j].wait()
        held[j] = mine + take[j]
        toward, away = (1, 3) if j < 2 else (3, 1)
        far.append(net.send(part(j, 2), lands.at[0, j], "x", toward))
        near.append(net.send(part(j, away), lands.at[1, j], "x", away))
    passing = []
    for j in range(4):
        toward = 1 if j < 2 else 3
        far[j].wait_recv()
        lands[0, j] = lands[0, j] + part(j, toward)[...]
        passing.append(net.send(lands.at[0, j], lands.at[2, j], "x", toward))
    for j in range(4):
        near[j].wait_recv()
        passing[j].wait_recv()
        at = 512 + 256 * j if j < 2 else 256 * j - 512
        both[k, :, at : at + 256] = part(j, 0)[...] + lands[1, j] + lands[2, j]
    copy = net.send(both.at[k], both.at[k], "core")
    for other in far + near + passing:
        other.wait_send()
    copy.wait()
    flat = both[...].reshape(160, 1024)
    view = both[:, :, pl.ds(pl.multiple_of(512 * k, 512), 512)].reshape(160, 512)
    side = both[:, :, pl.ds(pl.multiple_of(512 + 256 * k, 256), 256)].reshape(160, 256)
    gram = dotf(view.T, view, 1, 0)
    for t, (i, j) in enumerate(UPPER):
        source[128 * t : 128 * t + 128] = gram[128 * i : 128 * i + 128, 128 * j : 128 * j + 128]
    crossed = dotf(flat[:, 0:512].T, side, 1, 0)
    for j in range(2):
        for i in range(4):
            t = 10 + 4 * j + i
            source[128 * t : 128 * t + 128] = crossed[128 * i : 128 * i + 128, 128 * j : 128 * j + 128]
    together(
        [
            gram_stream(net, axes, source.at[first : first + rows], *buffers)
            for (axes, first, rows), buffers in zip(GRAMS, grams)
        ]
    )
    for (_, first, rows), buffers in zip(GRAMS, grams):
        s1, s2, r2 = buffers[7].shape[:3]
        for i in range(s1):
            for j in range(s2):
                at = first + r2 * (s2 * i + j)
                source[at : at + r2] = buffers[7][i, j]

    full[k * 4 + x] = both[k]
    full[(1 - k) * 4 + x] = both[1 - k]
    here = full.at[k * 4 + x]
    across = [net.send(here, here, "x", s) for s in (2, 1, 3)]
    scale = 1.0 / people
    a_ref[:, 0:512] = jnp.zeros((512, 512), F32)
    for t, (i, j) in enumerate(UPPER):
        a_ref[128 * i : 128 * i + 128, 128 * j : 128 * j + 128] = source[128 * t : 128 * t + 128] * scale
    for j in range(2):
        at = pl.ds(pl.multiple_of(256 * k + 128 * j, 128), 128)
        for i in range(4):
            t = 10 + 4 * j + i
            cross[128 * i : 128 * i + 128, at] = source[128 * t : 128 * t + 128] * scale
    pair = [net.send(cross.at[:, cols], cross.at[:, cols], "core")]
    swaps = []
    for i in range(4):
        block = (slice(128 * i, 128 * i + 128), slice(0, 128 * i + 128))
        swaps.append(net.plan(inv.at[(k, *block)], inv.at[(k, *block)], "core"))
        if i < 3:
            rest = slice(128 * i + 128, 512)
            for v in range(2):
                inv[v, 128 * i : 128 * i + 128, rest] = jnp.zeros((128, 384 - 128 * i), F32)

    def done(i):
        block = (slice(128 * i, 128 * i + 128), slice(0, 128 * i + 128))
        inv[(k, *block)] = a_ref[128 * i : 128 * i + 128, 512 : 640 + 128 * i]
        swaps[i].start()

    invert(a_ref, d_ref, done)
    for s, copy in zip((2, 1, 3), across):
        copy.wait()
        came = full.at[k * 4 + place.other("x", -s)]
        pair.append(net.send(came, came, "core"))
    finish(swaps)
    pair[0].wait()
    left = unit(dotf(dotf(dotf(init[...].T, inv[1], 1, 0), cross[...], 1, 1), inv[0], 1, 1))
    scale = 1.0 / math.sqrt(inv.shape[1])
    geno_weights = dotf(left, inv[0], 1, 0)
    right = unit(dotf(dotf(geno_weights, cross[...], 1, 0), inv[1], 1, 1))
    trait_weights = dotf(right, inv[1], 1, 0)
    finish(pair[1:])
    flat = full[...].reshape(640, 1024)
    tscore = dotf(flat[:, 512:1024], trait_weights * scale, 1, 1).astype(jnp.bfloat16)
    trait_t = tscore.T

    def put(target, at, lhs, rhs):
        width = rhs.shape[1]
        target[:, :, :, at : at + width] = jnp.dot(lhs, rhs, preferred_element_type=F32).reshape(
            4, 8, 8, width
        )

    scores[:, 256:512] = tscore
    running = {}
    geno_t = None
    for turn in TURNS:
        if turn not in running:
            make, _, first, count, genos = STREAMS[turn]
            target = parts[turn][0]
            for at in range(0, count, 256):
                put(target, at, trait_t, traits[:, first + at : first + at + 256])
            if genos:
                gscore = dotf(flat[:, 0:512], geno_weights * scale, 1, 1).astype(jnp.bfloat16)
                scores[:, 0:256] = gscore
                geno_t = gscore.T
            for at in range(0, genos, 256):
                put(target, count + at, geno_t, std[:, at : at + 256])
            running[turn] = make(net, *parts[turn])
        next(running[turn], None)
    together(running.values())
    scale = 1.0 / math.sqrt(people)
    for (_, _, first, count, genos), part_of in zip(STREAMS, parts):
        loads[:, 512 + first : 512 + first + count] = part_of[4][:, 0:count] * scale
        if genos:
            loads[:, 0:512] = part_of[4][:, count : count + genos] * scale


def cca(people, geno, freq, traits, gsk, tsk, init):
    vm, far = pl.BlockSpec(memory_space=pltpu.VMEM), pl.BlockSpec(memory_space=pl.ANY)
    sems = 4 + 12 + 1 + 3 * (2 * (3 + 3 + 7)) + 3 + 1 + 4 + 3 + (6 + 14) + (6 + 7) + 2 * (14 + 3)
    return pl.pallas_call(
        functools.partial(cca_kernel, people),
        out_shape=[
            jax.ShapeDtypeStruct((640, 512), jnp.bfloat16),
            jax.ShapeDtypeStruct((8, 4608), F32),
        ],
        in_specs=[far, vm, far, far, far, vm],
        out_specs=[vm] * 2,
        scratch_shapes=[
            pltpu.VMEM((640, 512), jnp.int32),
            pltpu.VMEM((640, 4096), jnp.bfloat16),
            pltpu.VMEM((512, 512), jnp.bfloat16),
            pltpu.VMEM((4096, 512), jnp.bfloat16),
            pltpu.VMEM((640, 512), jnp.bfloat16),
            pltpu.VMEM((4, 320, 256), F32),
            pltpu.VMEM((4, 320, 256), F32),
            pltpu.VMEM((4, 320, 256), F32),
            pltpu.VMEM((3, 4, 80, 256), F32),
            pltpu.VMEM((2, 80, 1024), F32),
            pltpu.VMEM((2304, 128), F32),
            *[buffer for axes, _, rows in GRAMS for buffer in gram_scratch(axes, rows)],
            pltpu.VMEM((512, 1024), F32),
            pltpu.VMEM((128, 256), F32),
            pltpu.VMEM((2, 512, 512), F32),
            pltpu.VMEM((512, 512), F32),
            pltpu.VMEM((8, 80, 1024), F32),
            *[buffer for _, scratch, _, count, genos in STREAMS for buffer in scratch(count + genos)],
            pltpu.SemaphoreType.DMA((sems,)),
            pltpu.SemaphoreType.DMA((sems,)),
            pltpu.SemaphoreType.DMA((6,)),
        ],
        compiler_params=pltpu.CompilerParams(
            collective_id=1, has_side_effects=True, vmem_limit_bytes=60 << 20
        ),
        name="cca",
    )(geno, freq, traits, gsk, tsk, init)


def on_device(genotypes, frequencies, traits, geno_sketch, trait_sketch, initial):
    people = genotypes.shape[0] * lax.axis_size("rows")
    scores, loads = cca(
        people, genotypes, frequencies[None, :], traits, geno_sketch, trait_sketch, initial
    )
    pairs, width = initial.shape[1], genotypes.shape[1]
    return (scores[:, :pairs], scores[:, pairs:], loads[:, :width], loads[:, width:])


def solution(mesh):
    placed = (
        P("rows", "cols"),
        P("cols"),
        P("rows", "cols"),
        P("cols", None),
        P("cols", None),
        P(),
    )
    return jax.shard_map(
        on_device,
        mesh=mesh,
        in_specs=placed,
        out_specs=(P("rows", None), P("rows", None), P("rows", "cols"), P("rows", "cols")),
        check_vma=False,
    )
```
